32 devices in a mesh: ctx: 4 (over y, x), dp: 8 (over z, core).
Axes of the slice: x: 2, y: 2, z: 4, core: 2. Of those that a mesh axis runs over, the one named last changes fastest.
Arguments:
- queries: bfloat16 [8, 512, 2048], P('dp', 'ctx'), may hold values from -64 to 64
- keys: bfloat16 [8, 512, 1024], P('dp', 'ctx'), may hold values from -64 to 64
- values: bfloat16 [8, 512, 1024], P('dp', 'ctx'), may hold values from -6 to 6
- grad_out: bfloat16 [8, 512, 2048], P('dp', 'ctx'), may hold values from -40 to 40
- query_gain: float32 [128], replicated, may hold values from 0.5 to 6.5
- key_gain: float32 [128], replicated, may hold values from 0.5 to 6.5
- doc_lengths: int32 [8, 4], P('dp'), may hold values from 1 to 256, 512 in all within a row
Outputs:
- query_grad: bfloat16 [8, 512, 2048], P('dp', 'ctx')
- key_gradient: bfloat16 [8, 512, 1024], P('dp', 'ctx')
- value_gradient: bfloat16 [8, 512, 1024], P('dp', 'ctx')
- query_gain_grad: float32 [128], replicated
- key_gain_grad: float32 [128], replicated
The draws below stay inside these ranges and needn't reach their ends.
Inputs may be any that keep to these rules, and one draw needn't show every extreme that they name: `doc_lengths`: each row sums to 512.
All inputs are finite; a program needn't handle non-finite values.
Results may differ from the reference program's by a relative error of at most 0.024.
The reference program's roundings to bfloat16 on the way count: a program that leaves them out, or rounds other values in their place, can miss the bound.
Values may be sent and summed in bfloat16 or wider, within the bound.
No kernel may reach another device: no remote copies, remote signals or barrier semaphores. Data moves between devices by JAX's collectives and lax.ppermute only.
A program may use at most 64 MiB of HBM per device.

```python
import math
import jax
import jax.numpy as jnp
import numpy as np
from jax import lax

QUERY_HEADS = 16
KEY_VALUE_HEADS = 8
HEAD_SIZE = 128
WINDOW_SIZE = 256
NDOCS = 4
TOK_DEV = 128
SEQUENCE_LENGTH = 512
SEQUENCE_COUNT = 8


def draw_keys(key, part):
    return jnp.clip(jax.random.normal(jax.random.fold_in(key, 106), (SEQUENCE_COUNT, SEQUENCE_LENGTH, KEY_VALUE_HEADS * HEAD_SIZE), jnp.float32), -6.0, 6.0).astype(jnp.bfloat16)


def draw_queries(key, part):
    array_shape = (SEQUENCE_COUNT, SEQUENCE_LENGTH, QUERY_HEADS * HEAD_SIZE)
    return jnp.clip(jax.random.normal(jax.random.fold_in(key, 116), array_shape, jnp.float32), -6.0, 6.0).astype(jnp.bfloat16)


def draw_grad_out(key, part):
    array_shape = (SEQUENCE_COUNT, SEQUENCE_LENGTH, QUERY_HEADS * HEAD_SIZE)
    ramp = 1.0 + 2.0 * jnp.arange(SEQUENCE_LENGTH, dtype=jnp.float32)[None, :, None] / (SEQUENCE_LENGTH - 1)
    return (jnp.clip(jax.random.normal(jax.random.fold_in(key, 123), array_shape, jnp.float32), -6.0, 6.0) * ramp).astype(jnp.bfloat16)


def draw_query_gain(key, part):
    return jax.random.uniform(jax.random.fold_in(key, 132), (HEAD_SIZE,), jnp.float32, 0.5, 1.5)


def draw_key_gain(key, part):
    return jax.random.uniform(jax.random.fold_in(key, 142), (HEAD_SIZE,), jnp.float32, 0.5, 1.5)


def levels(stream_key, shape, shards, smallest, high):
    def one(axis_at, blocks):
        heights = jax.random.uniform(jax.random.fold_in(jax.random.fold_in(stream_key, 6), axis_at), (blocks,), jnp.float32, smallest / len(shards), high / len(shards))
        return jnp.repeat(jnp.exp(heights), shape[axis_at] // blocks).reshape((-1,) + (1,) * (len(shape) - axis_at - 1))

    level = one(*shards[0])
    for cut in shards[1:]:
        level = level * one(*cut)
    return level


def split_up(count, total, limit, skew):
    loads = [(1 << 20) // math.isqrt(standing ** skew) + 1 for standing in range(2, count + 1)]
    surplus, holding = total - limit - (count - 1), [1] * (count - 1)
    while surplus > 0:
        free = [i for i in range(count - 1) if holding[i] < limit]
        whole, remaining = sum([loads[i] for i in free]), surplus
        for i in free:
            extra = min(limit - holding[i], max(1, remaining * loads[i] // whole), surplus)
            holding[i] = holding[i] + extra
            surplus = surplus - extra
    return np.array([limit] + holding)


def ragged(stream_key, amount, total, limit, skew):
    if amount == 2:
        one = jax.random.randint(stream_key, (), max(1, total - limit), min(limit, total - 1) + 1)
        return jnp.stack([one, total - one])
    sizes = jnp.asarray(split_up(amount, total, limit, skew), jnp.int32)
    couples = (amount - 1) // 2
    donor, sink = sizes[1:1 + 2 * couples:2], sizes[2:2 + 2 * couples:2]
    slack = jnp.minimum(donor - 1, limit - sink)
    moved = jax.random.randint(jax.random.fold_in(stream_key, 1), (couples,), 0, 1 << 20) % (slack + 1)
    sizes = sizes.at[1:1 + 2 * couples:2].set(donor - moved).at[2:2 + 2 * couples:2].set(sink + moved)
    return sizes[jax.random.permutation(jax.random.fold_in(stream_key, 2), amount)]


def normal_values(rng, extent, spread, reach, split=(), kind=jnp.bfloat16):
    array = spread * jax.random.normal(rng, extent, jnp.float32)
    if split:
        array = array * levels(rng, extent, split, -0.22, 0.18)
    return jnp.clip(array, -reach, reach).astype(kind)


def setup_inputs(seed: int = 0) -> dict:
    key_list = jax.random.split(jax.random.key(seed), 8)
    queries = draw_queries(jax.random.fold_in(key_list[7], 71), 0)
    keys = draw_keys(jax.random.fold_in(key_list[7], 71), 0)
    values = normal_values(key_list[2], (SEQUENCE_COUNT, SEQUENCE_LENGTH, KEY_VALUE_HEADS * HEAD_SIZE), 1.0, 6.0, ((0, 8), (1, 4)))
    grad_out = draw_grad_out(jax.random.fold_in(key_list[7], 71), 0)
    query_gain = draw_query_gain(jax.random.fold_in(key_list[7], 71), 0)
    key_gain = draw_key_gain(jax.random.fold_in(key_list[7], 71), 0)
    doc_lengths = jax.vmap(lambda own: ragged(own, NDOCS, SEQUENCE_LENGTH, SEQUENCE_LENGTH // 2, 2))(jax.random.split(key_list[6], SEQUENCE_COUNT)).reshape((SEQUENCE_COUNT, NDOCS)).astype(jnp.int32)
    return dict(queries=queries, keys=keys, values=values, grad_out=grad_out, query_gain=query_gain, key_gain=key_gain, doc_lengths=doc_lengths)


norm_epsilon = 1e-06
score_scale = 168.0 ** (-0.5)

def rms_gain(x, gain):
    inverse = lax.rsqrt(lax.optimization_barrier(jnp.mean(x * x, axis=-1, keepdims=True)) + norm_epsilon)
    return x * inverse * gain

def doc_index(lengths_row, positions):
    ends = jnp.cumsum(lengths_row).astype(jnp.int32)
    hits = (positions[:, None] >= ends[None, :]).astype(jnp.int32)
    return lax.optimization_barrier(jnp.sum(hits, axis=1)).astype(jnp.int32)

def block_grads(query_n, key_n, value_blk, grad_blk, allowed):
    query_f = query_n.astype(jnp.float32)
    key_f = key_n.astype(jnp.float32)
    value_f = value_blk.astype(jnp.float32)
    grad_f = grad_blk.astype(jnp.float32)
    scores = jnp.einsum('qhgd,khd->hgqk', query_f, key_f) * score_scale
    scores = jnp.where(allowed[None, None], scores, -jnp.inf)
    row_max = lax.optimization_barrier(jnp.max(scores, axis=-1, keepdims=True))
    weights = jnp.exp(scores - row_max)
    probs = weights / lax.optimization_barrier(jnp.sum(weights, axis=-1, keepdims=True))
    probs_low = lax.optimization_barrier(probs.astype(jnp.bfloat16)).astype(jnp.float32)
    attended = jnp.einsum('hgqk,khd->qhgd', probs_low, value_f).astype(jnp.bfloat16)
    attended = lax.optimization_barrier(attended).astype(jnp.float32)
    delta = lax.optimization_barrier(jnp.sum(grad_f * attended, axis=-1))
    dprobs = jnp.einsum('qhgd,khd->hgqk', grad_f, value_f)
    dscores = probs * (dprobs - jnp.transpose(delta, (1, 2, 0))[..., None])
    dscores = lax.optimization_barrier(dscores.astype(jnp.bfloat16)).astype(jnp.float32)
    dquery = jnp.einsum('hgqk,khd->qhgd', dscores, key_f) * score_scale
    dkey = jnp.einsum('hgqk,qhgd->khd', dscores, query_f) * score_scale
    dvalue = jnp.einsum('hgqk,qhgd->khd', probs_low, grad_f)
    return (dquery, dkey, dvalue)

def reference(queries, keys, values, grad_out, query_gain, key_gain, doc_lengths):
    query_group_count = QUERY_HEADS // KEY_VALUE_HEADS
    key_window_span = WINDOW_SIZE + TOK_DEV

    def one_sequence(items):
        query_sequence, key_sequence, value_sequence, sequence_gradient, lengths_row = items
        positions = jnp.arange(SEQUENCE_LENGTH, dtype=jnp.int32)
        documents = doc_index(lengths_row, positions)
        unnormed_query = query_sequence.astype(jnp.float32).reshape(SEQUENCE_LENGTH, KEY_VALUE_HEADS, query_group_count, HEAD_SIZE)
        unnormed_key = key_sequence.astype(jnp.float32).reshape(SEQUENCE_LENGTH, KEY_VALUE_HEADS, HEAD_SIZE)
        query_normed = rms_gain(unnormed_query, query_gain).astype(jnp.bfloat16)
        normed_key = rms_gain(unnormed_key, key_gain).astype(jnp.bfloat16)
        head_gradients = sequence_gradient.reshape(SEQUENCE_LENGTH, KEY_VALUE_HEADS, query_group_count, HEAD_SIZE)
        key_rows_padded = jnp.concatenate([jnp.zeros((WINDOW_SIZE, KEY_VALUE_HEADS, HEAD_SIZE), jnp.bfloat16), normed_key], axis=0)
        value_rows_padded = jnp.concatenate([jnp.zeros((WINDOW_SIZE, KEY_VALUE_HEADS, HEAD_SIZE), jnp.bfloat16), value_sequence.reshape(SEQUENCE_LENGTH, KEY_VALUE_HEADS, HEAD_SIZE)], axis=0)
        padded_pos = jnp.arange(SEQUENCE_LENGTH + WINDOW_SIZE, dtype=jnp.int32) - WINDOW_SIZE
        padded_docs = jnp.concatenate([jnp.full((WINDOW_SIZE,), -1, jnp.int32), documents], axis=0)

        def step(carry, index):
            sum_keys, value_sums = carry
            first_pos = (index * TOK_DEV).astype(jnp.int32)
            query_blk = lax.dynamic_slice_in_dim(query_normed, first_pos, TOK_DEV, 0)
            grad_blk = lax.dynamic_slice_in_dim(head_gradients, first_pos, TOK_DEV, 0)
            key_blk = lax.dynamic_slice_in_dim(key_rows_padded, first_pos, key_window_span, 0)
            value_blk = lax.dynamic_slice_in_dim(value_rows_padded, first_pos, key_window_span, 0)
            key_pos = lax.dynamic_slice_in_dim(padded_pos, first_pos, key_window_span, 0)
            key_docs = lax.dynamic_slice_in_dim(padded_docs, first_pos, key_window_span, 0)
            query_pos = lax.dynamic_slice_in_dim(positions, first_pos, TOK_DEV, 0)
            query_docs = lax.dynamic_slice_in_dim(documents, first_pos, TOK_DEV, 0)
            allowed = (key_docs[None, :] == query_docs[:, None]) & (key_pos[None, :] <= query_pos[:, None]) & (query_pos[:, None] - key_pos[None, :] < WINDOW_SIZE)
            dquery, dkey, dvalue = block_grads(query_blk, key_blk, value_blk, grad_blk, allowed)
            dkey = jnp.concatenate([lax.optimization_barrier(dkey[:WINDOW_SIZE].astype(jnp.bfloat16)).astype(jnp.float32), dkey[WINDOW_SIZE:]], axis=0)
            dvalue = jnp.concatenate([lax.optimization_barrier(dvalue[:WINDOW_SIZE].astype(jnp.bfloat16)).astype(jnp.float32), dvalue[WINDOW_SIZE:]], axis=0)
            sum_keys = lax.dynamic_update_slice_in_dim(sum_keys, lax.dynamic_slice_in_dim(sum_keys, first_pos, key_window_span, 0) + dkey, first_pos, 0)
            value_sums = lax.dynamic_update_slice_in_dim(value_sums, lax.dynamic_slice_in_dim(value_sums, first_pos, key_window_span, 0) + dvalue, first_pos, 0)
            return ((sum_keys, value_sums), dquery)
        initial_sums = (jnp.zeros((SEQUENCE_LENGTH + WINDOW_SIZE, KEY_VALUE_HEADS, HEAD_SIZE), jnp.float32), jnp.zeros((SEQUENCE_LENGTH + WINDOW_SIZE, KEY_VALUE_HEADS, HEAD_SIZE), jnp.float32))
        (sum_keys, value_sums), query_block_gradients = lax.scan(step, initial_sums, jnp.arange(SEQUENCE_LENGTH // TOK_DEV, dtype=jnp.int32))
        query_normed_gradient = query_block_gradients.reshape(SEQUENCE_LENGTH, KEY_VALUE_HEADS, query_group_count, HEAD_SIZE)
        unused_q, back_query = jax.vjp(rms_gain, unnormed_query, query_gain)
        query_raw_gradient, query_gain_gradient = back_query(query_normed_gradient)
        unused_k, backward_key = jax.vjp(rms_gain, unnormed_key, key_gain)
        key_raw_gradient, key_gain_gradient = backward_key(sum_keys[WINDOW_SIZE:])
        return (query_raw_gradient.astype(jnp.bfloat16).reshape(SEQUENCE_LENGTH, QUERY_HEADS * HEAD_SIZE), key_raw_gradient.astype(jnp.bfloat16).reshape(SEQUENCE_LENGTH, KEY_VALUE_HEADS * HEAD_SIZE), value_sums[WINDOW_SIZE:].astype(jnp.bfloat16).reshape(SEQUENCE_LENGTH, KEY_VALUE_HEADS * HEAD_SIZE), query_gain_gradient, key_gain_gradient)
    query_grad, key_gradient, value_gradient, query_gains, key_gains = lax.map(one_sequence, (queries, keys, values, grad_out, doc_lengths))
    return (query_grad, key_gradient, value_gradient, lax.optimization_barrier(jnp.sum(query_gains, axis=0)), lax.optimization_barrier(jnp.sum(key_gains, axis=0)))
```

```python
import functools

import jax
import jax.numpy as jnp
from jax import lax
from jax.experimental import pallas as pl
from jax.experimental.pallas import tpu as pltpu
from jax.sharding import PartitionSpec as P

QUERY_HEADS = 16
KEY_VALUE_HEADS = 8
HEAD_SIZE = 128
WINDOW_SIZE = 256
GROUP = QUERY_HEADS // KEY_VALUE_HEADS

norm_epsilon = 1e-06
score_scale = 168.0 ** (-0.5)
MASKED = -1e30


F32 = jnp.float32
BF16 = jnp.bfloat16


def dot(a, b, ca, cb):
    return lax.dot_general(a, b, (((ca,), (cb,)), ((), ())), preferred_element_type=F32)


def inverse_rms(x):
    return lax.rsqrt(jnp.mean(x * x, axis=-1, keepdims=True) + norm_epsilon)


def document_of(lengths_ref, positions):
    index = jnp.zeros(positions.shape, jnp.int32)
    end = jnp.int32(0)
    for doc in range(lengths_ref.shape[1]):
        end = end + lengths_ref[0, doc]
        index = index + (positions >= end).astype(jnp.int32)
    return index


def mask_bias(lengths_ref, first, keys, rows):
    key_pos = first - WINDOW_SIZE + lax.broadcasted_iota(jnp.int32, (keys, 1), 0)
    query_pos = first + lax.broadcasted_iota(jnp.int32, (1, rows), 1)
    key_doc = jnp.where(key_pos >= 0, document_of(lengths_ref, key_pos), -1)
    query_doc = document_of(lengths_ref, query_pos)
    gap = query_pos - key_pos
    allowed = (key_doc == query_doc) & (gap >= 0) & (gap < WINDOW_SIZE)
    return jnp.where(allowed, 0.0, MASKED).astype(F32)


def main_kernel(
    first_ref, lengths_ref,
    q_ref, k0_ref, k1_ref, k2_ref, v0_ref, v1_ref, v2_ref, go_ref, qg_ref, kg_ref,
    dq_ref, g1k_ref, g1v_ref, g2k_ref, g2v_ref, dk_ref, dv_ref, gains_ref,
    bias_ref,
):
    rows = q_ref.shape[0]
    keys = WINDOW_SIZE + rows

    @pl.when(pl.program_id(0) == 0)
    def _():
        bias_ref[...] = mask_bias(lengths_ref, first_ref[0], keys, rows)
        gains_ref[...] = jnp.zeros_like(gains_ref)

    q_gain = qg_ref[...]
    k_gain = kg_ref[...]
    q = jnp.concatenate([q_ref[:, i * HEAD_SIZE:(i + 1) * HEAD_SIZE] for i in range(GROUP)], axis=0).astype(F32)
    go = jnp.concatenate([go_ref[:, i * HEAD_SIZE:(i + 1) * HEAD_SIZE] for i in range(GROUP)], axis=0)
    q_inv = inverse_rms(q)
    q_hat = q * q_inv
    qn = (q_hat * q_gain).astype(BF16)
    k = jnp.concatenate([k2_ref[...], k1_ref[...], k0_ref[...]], axis=0).astype(F32)
    k_hat = k * inverse_rms(k)
    kn = (k_hat * k_gain).astype(BF16)
    v = jnp.concatenate([v2_ref[...], v1_ref[...], v0_ref[...]], axis=0)

    bias = bias_ref[...]
    s = dot(kn, qn, 1, 1) * score_scale + jnp.concatenate([bias] * GROUP, axis=1)
    e = jnp.exp(s - jnp.max(s, axis=0, keepdims=True))
    p = e * (1.0 / jnp.sum(e, axis=0, keepdims=True))
    p_low = p.astype(BF16)
    attended_t = dot(v, p_low, 0, 0).astype(BF16).astype(F32)
    go_t = jnp.transpose(go.astype(F32))
    delta = jnp.sum(go_t * attended_t, axis=0, keepdims=True)
    dp = dot(v, go, 1, 1)
    ds = (p * (dp - delta)).astype(BF16)
    dk = dot(ds, qn, 1, 0) * score_scale
    dv = dot(p_low, go, 1, 0)
    dqn = dot(ds, kn, 0, 0) * score_scale

    g2k = dk[:rows].astype(BF16)
    g1k = dk[rows:2 * rows].astype(BF16)
    g2k_ref[...] = g2k
    g1k_ref[...] = g1k
    dk_ref[...] = dk[2 * rows:]
    g2v_ref[...] = dv[:rows].astype(BF16)
    g1v_ref[...] = dv[rows:2 * rows].astype(BF16)
    dv_ref[...] = dv[2 * rows:]

    k_part = (
        jnp.sum(g2k.astype(F32) * k_hat[:rows], axis=0, keepdims=True)
        + jnp.sum(g1k.astype(F32) * k_hat[rows:2 * rows], axis=0, keepdims=True)
        + jnp.sum(dk[2 * rows:] * k_hat[2 * rows:], axis=0, keepdims=True)
    )
    q_part = jnp.sum(dqn * q_hat, axis=0, keepdims=True)
    gains_ref[0:1, :] += q_part
    gains_ref[1:2, :] += k_part

    t = dqn * q_gain
    dq = (q_inv * (t - q_hat * jnp.mean(t * q_hat, axis=-1, keepdims=True))).astype(BF16)
    for i in range(GROUP):
        dq_ref[:, i * HEAD_SIZE:(i + 1) * HEAD_SIZE] = dq[i * rows:(i + 1) * rows]


def attention(first, lengths, q, ks, vs, go, q_gain, k_gain):
    rows = q.shape[0]
    wide = pl.BlockSpec((rows, GROUP * HEAD_SIZE), lambda g, *_: (0, g))
    slim = pl.BlockSpec((rows, HEAD_SIZE), lambda g, *_: (0, g))
    gain = pl.BlockSpec((1, HEAD_SIZE), lambda g, *_: (0, 0))
    kv_shape = (rows, KEY_VALUE_HEADS * HEAD_SIZE)
    sds = jax.ShapeDtypeStruct
    return pl.pallas_call(
        main_kernel,
        grid_spec=pltpu.PrefetchScalarGridSpec(
            num_scalar_prefetch=2,
            grid=(KEY_VALUE_HEADS,),
            in_specs=[wide] + [slim] * 6 + [wide, gain, gain],
            out_specs=[wide] + [slim] * 6 + [pl.BlockSpec((8, HEAD_SIZE), lambda g, *_: (0, 0))],
            scratch_shapes=[pltpu.VMEM((WINDOW_SIZE + rows, rows), F32)],
        ),
        out_shape=[sds(q.shape, BF16)] + [sds(kv_shape, BF16)] * 4 + [sds(kv_shape, F32)] * 2 + [sds((8, HEAD_SIZE), F32)],
        name="attention",
    )(first, lengths, q, *ks, *vs, go, q_gain, k_gain)


def final_kernel(odd_ref, k_ref, dk_ref, dv_ref, ak_ref, av_ref, bk_ref, bv_ref, kg_ref, ko_ref, vo_ref):
    keep = (odd_ref[0] == 0).astype(F32)
    k_gain = kg_ref[...]
    vo_ref[...] = (dv_ref[...] + av_ref[...].astype(F32) * keep + bv_ref[...].astype(F32)).astype(BF16)
    for h in range(KEY_VALUE_HEADS):
        cols = slice(h * HEAD_SIZE, (h + 1) * HEAD_SIZE)
        total = dk_ref[:, cols] + ak_ref[:, cols].astype(F32) * keep + bk_ref[:, cols].astype(F32)
        k = k_ref[:, cols].astype(F32)
        inv = inverse_rms(k)
        k_hat = k * inv
        t = total * k_gain
        ko_ref[:, cols] = (inv * (t - k_hat * jnp.mean(t * k_hat, axis=-1, keepdims=True))).astype(BF16)


def finish(odd, k, dk, dv, ak, av, bk, bv, k_gain):
    vmem = pl.BlockSpec(memory_space=pltpu.VMEM)
    return pl.pallas_call(
        final_kernel,
        in_specs=[pl.BlockSpec(memory_space=pltpu.SMEM)] + [vmem] * 8,
        out_specs=[vmem] * 2,
        out_shape=[jax.ShapeDtypeStruct(k.shape, BF16)] * 2,
        name="finish",
    )(odd, k, dk, dv, ak, av, bk, bv, k_gain)


def sum_over(x, axis):
    count, stride = lax.axis_size(axis), 1
    while stride < count:
        rest = count // stride
        radix = next(f for f in range(2, rest + 1) if rest % f == 0)
        def moved(turn):
            pairs = []
            for source in range(count):
                digit = source // stride % radix
                pairs.append((source, source + ((digit + turn) % radix - digit) * stride))
            return lax.ppermute(x, axis, pairs)
        x = x + sum([moved(turn) for turn in range(1, radix)])
        stride = stride * radix
    return x


def per_device(queries, keys, values, grad_out, query_gain, key_gain, doc_lengths):
    rows = queries.shape[1]
    count = lax.axis_size("ctx")
    assert rows * 2 == WINDOW_SIZE and count % 2 == 0
    here = lax.axis_index("ctx")
    odd = lax.rem(here, 2)
    first = (here * rows).astype(jnp.int32)
    q, k, v, go = queries[0], keys[0], values[0], grad_out[0]
    q_gain, k_gain = query_gain[None], key_gain[None]

    ahead = [(i, (i + 2) % count) for i in range(count)]
    behind = [(i, (i - 2) % count) for i in range(count)]
    swap = [(i, i ^ 1) for i in range(count)]

    k2 = lax.ppermute(k, "ctx", ahead)
    v2 = lax.ppermute(v, "ctx", ahead)
    k1 = lax.ppermute(jnp.where(odd == 1, k2, k), "ctx", swap)
    v1 = lax.ppermute(jnp.where(odd == 1, v2, v), "ctx", swap)

    dq, g1k, g1v, g2k, g2v, dk, dv, gains = attention(
        first[None], doc_lengths, q, (k, k1, k2), (v, v1, v2), go, q_gain, k_gain
    )

    keep = (odd == 1).astype(F32)
    ak = lax.ppermute(g1k, "ctx", swap)
    bk = lax.ppermute((g2k.astype(F32) + ak.astype(F32) * keep).astype(BF16), "ctx", behind)
    av = lax.ppermute(g1v, "ctx", swap)
    bv = lax.ppermute((g2v.astype(F32) + av.astype(F32) * keep).astype(BF16), "ctx", behind)
    gains = sum_over(sum_over(gains, "dp"), "ctx")

    dk, dv = finish(odd.astype(jnp.int32)[None], k, dk, dv, ak, av, bk, bv, k_gain)
    return (dq[None], dk[None], dv[None], gains[0], gains[1])


def solution(mesh):
    in_specs = (
        P("dp", "ctx", None),
        P("dp", "ctx", None),
        P("dp", "ctx", None),
        P("dp", "ctx", None),
        P(),
        P(),
        P("dp", None),
    )
    out_specs = (P("dp", "ctx", None), P("dp", "ctx", None), P("dp", "ctx", None), P(), P())
    return jax.shard_map(
        per_device, mesh=mesh, in_specs=in_specs, out_specs=out_specs, check_vma=False
    )
```

```python
import functools

import jax
import jax.numpy as jnp
from jax import lax
from jax.experimental import pallas as pl
from jax.experimental.pallas import tpu as pltpu
from jax.sharding import PartitionSpec as P

QUERY_HEADS = 16
KEY_VALUE_HEADS = 8
HEAD_SIZE = 128
WINDOW_SIZE = 256
GROUP = QUERY_HEADS // KEY_VALUE_HEADS

norm_epsilon = 1e-06
score_scale = 168.0 ** (-0.5)
MASKED = -1e30
LOG2E = 1.4426950408889634
UNROLL = 2


F32 = jnp.float32
BF16 = jnp.bfloat16


def dot(a, b, ca, cb):
    return lax.dot_general(a, b, (((ca,), (cb,)), ((), ())), preferred_element_type=F32)


def inverse_rms(x):
    return lax.rsqrt(jnp.mean(x * x, axis=-1, keepdims=True) + norm_epsilon)


def document_of(lengths_ref, positions):
    index = jnp.zeros(positions.shape, jnp.int32)
    end = jnp.int32(0)
    for doc in range(lengths_ref.shape[1]):
        end = end + lengths_ref[0, doc]
        index = index + (positions >= end).astype(jnp.int32)
    return index


def mask_bias(lengths_ref, first, keys, rows):
    key_pos = first - WINDOW_SIZE + lax.broadcasted_iota(jnp.int32, (keys, 1), 0)
    query_pos = first + lax.broadcasted_iota(jnp.int32, (1, rows), 1)
    key_doc = jnp.where(key_pos >= 0, document_of(lengths_ref, key_pos), -1)
    query_doc = document_of(lengths_ref, query_pos)
    gap = query_pos - key_pos
    allowed = (key_doc == query_doc) & (gap >= 0) & (gap < WINDOW_SIZE)
    return jnp.where(allowed, 0.0, MASKED).astype(F32)


def stacked(ref, u, rows):
    parts = [ref[:, (u * GROUP + i) * HEAD_SIZE:(u * GROUP + i + 1) * HEAD_SIZE] for i in range(GROUP)]
    return jnp.concatenate(parts, axis=0)


def columns(u):
    return slice(u * HEAD_SIZE, (u + 1) * HEAD_SIZE)


def prepare_kernel(first_ref, lengths_ref, q_ref, k_ref, v_ref, go_ref, qg_ref, kg_ref,
                   qn_ref, kn_ref, s_ref, dp_ref, got_ref, bias_ref, own_ref):
    rows = q_ref.shape[0]

    @pl.when(pl.program_id(0) == 0)
    def _():
        bias = mask_bias(lengths_ref, first_ref[0], WINDOW_SIZE + rows, rows)
        bias_ref[...] = bias[:WINDOW_SIZE]
        own_ref[...] = bias[WINDOW_SIZE:]

    bias = jnp.concatenate([own_ref[...]] * GROUP, axis=1)
    for u in range(UNROLL):
        q = stacked(q_ref, u, rows).astype(F32)
        go = stacked(go_ref, u, rows)
        qn = (q * inverse_rms(q) * qg_ref[...]).astype(BF16)
        k = k_ref[:, columns(u)].astype(F32)
        kn = (k * inverse_rms(k) * kg_ref[...]).astype(BF16)
        qn_ref[u] = qn
        kn_ref[:, columns(u)] = kn
        s_ref[u] = dot(kn, qn, 1, 1) * (score_scale * LOG2E) + bias
        dp_ref[u] = dot(v_ref[:, columns(u)], go, 1, 1)
        got_ref[u] = jnp.transpose(go)


def weigh_kernel(qn_ref, s_ref, bias_ref, k1_ref, k2_ref, go_ref, kg_ref, kn_ref, p_ref, g1v_ref, g2v_ref):
    rows = go_ref.shape[0]
    bias = jnp.concatenate([bias_ref[...]] * GROUP, axis=1)
    for u in range(UNROLL):
        k = jnp.concatenate([k2_ref[:, columns(u)], k1_ref[:, columns(u)]], axis=0).astype(F32)
        kn = (k * inverse_rms(k) * kg_ref[...]).astype(BF16)
        kn_ref[:, columns(u)] = kn
        s = dot(kn, qn_ref[u], 1, 1) * (score_scale * LOG2E) + bias
        s0 = s_ref[u]
        top = jnp.maximum(jnp.max(s, axis=0, keepdims=True), jnp.max(s0, axis=0, keepdims=True))
        e, e0 = jnp.exp2(s - top), jnp.exp2(s0 - top)
        inv = 1.0 / (jnp.sum(e, axis=0, keepdims=True) + jnp.sum(e0, axis=0, keepdims=True))
        p = e * inv
        p_ref[u, :WINDOW_SIZE] = p
        p_ref[u, WINDOW_SIZE:] = e0 * inv
        g = dot(p.astype(BF16), stacked(go_ref, u, rows), 1, 0).astype(BF16)
        g2v_ref[:, columns(u)] = g[:rows]
        g1v_ref[:, columns(u)] = g[rows:]


def score_kernel(p_ref, v0_ref, v1_ref, v2_ref, go_ref, got_ref, dp_ref, qn_ref, ds_ref, g1k_ref, g2k_ref):
    rows = go_ref.shape[0]
    for u in range(UNROLL):
        v = jnp.concatenate([v2_ref[:, columns(u)], v1_ref[:, columns(u)]], axis=0)
        p, p0 = p_ref[u, :WINDOW_SIZE], p_ref[u, WINDOW_SIZE:]
        attended = dot(v, p.astype(BF16), 0, 0) + dot(v0_ref[:, columns(u)], p0.astype(BF16), 0, 0)
        attended = attended.astype(BF16).astype(F32)
        delta = jnp.sum(got_ref[u].astype(F32) * attended, axis=0, keepdims=True)
        ds = (p * (dot(v, stacked(go_ref, u, rows), 1, 1) - delta)).astype(BF16)
        ds_ref[u, :WINDOW_SIZE] = ds
        ds_ref[u, WINDOW_SIZE:] = (p0 * (dp_ref[u] - delta)).astype(BF16)
        g = (dot(ds, qn_ref[u], 1, 0) * score_scale).astype(BF16)
        g2k_ref[:, columns(u)] = g[:rows]
        g1k_ref[:, columns(u)] = g[rows:]


def rest_kernel(q_ref, qn_ref, knx_ref, kn0_ref, ds_ref, p_ref, go_ref, qg_ref, kg_ref, dq_ref, dk_ref, dv_ref, gains_ref):
    rows = q_ref.shape[0]

    @pl.when(pl.program_id(0) == 0)
    def _():
        gains_ref[...] = jnp.zeros_like(gains_ref)

    for u in range(UNROLL):
        qn, ds = qn_ref[u], ds_ref[u]
        kn = jnp.concatenate([knx_ref[:, columns(u)], kn0_ref[:, columns(u)]], axis=0)
        dqn = dot(ds, kn, 0, 0) * score_scale
        dk_ref[:, columns(u)] = dot(ds[WINDOW_SIZE:], qn, 1, 0) * score_scale
        dv_ref[:, columns(u)] = dot(p_ref[u].astype(BF16), stacked(go_ref, u, rows), 1, 0)
        q = stacked(q_ref, u, rows).astype(F32)
        q_inv = inverse_rms(q)
        q_hat = q * q_inv
        gains_ref[0:1, :] += jnp.sum(dqn * q_hat, axis=0, keepdims=True)
        gains_ref[1:2, :] += jnp.sum(dqn * qn.astype(F32), axis=0, keepdims=True) / kg_ref[...]
        t = dqn * qg_ref[...]
        dq = (q_inv * (t - q_hat * jnp.mean(t * q_hat, axis=-1, keepdims=True))).astype(BF16)
        for i in range(GROUP):
            dq_ref[:, columns(u * GROUP + i)] = dq[i * rows:(i + 1) * rows]


def value_kernel(dv_ref, a_ref, b_ref, out_ref):
    out_ref[...] = (dv_ref[...] + a_ref[...].astype(F32) + b_ref[...].astype(F32)).astype(BF16)


def key_kernel(odd_ref, k_ref, dk_ref, a_ref, b_ref, kg_ref, out_ref):
    keep = (odd_ref[0] == 0).astype(F32)
    for h in range(k_ref.shape[1] // HEAD_SIZE):
        total = dk_ref[:, columns(h)] + a_ref[:, columns(h)].astype(F32) * keep + b_ref[:, columns(h)].astype(F32)
        k = k_ref[:, columns(h)].astype(F32)
        inv = inverse_rms(k)
        k_hat = k * inv
        t = total * kg_ref[...]
        out_ref[:, columns(h)] = (inv * (t - k_hat * jnp.mean(t * k_hat, axis=-1, keepdims=True))).astype(BF16)


def specs(rows):
    wide = pl.BlockSpec((rows, UNROLL * GROUP * HEAD_SIZE), lambda g, *_: (0, g))
    slim = pl.BlockSpec((rows, UNROLL * HEAD_SIZE), lambda g, *_: (0, g))
    gain = pl.BlockSpec((1, HEAD_SIZE), lambda g, *_: (0, 0))

    def per(height, width, at=0):
        return pl.BlockSpec((UNROLL, height, width), lambda g, *_: (g, at, 0))

    return wide, slim, gain, per


def call(kernel, name, in_specs, outs, args, scalars=(), scratch=()):
    out_specs = [spec for spec, _, _ in outs]
    return pl.pallas_call(
        kernel,
        grid_spec=pltpu.PrefetchScalarGridSpec(
            num_scalar_prefetch=len(scalars),
            grid=(KEY_VALUE_HEADS // UNROLL,),
            in_specs=in_specs,
            out_specs=out_specs,
            scratch_shapes=scratch,
        ),
        out_shape=[jax.ShapeDtypeStruct(shape, kind) for _, shape, kind in outs],
        name=name,
    )(*scalars, *args)


def sum_over(x, axis):
    count, stride = lax.axis_size(axis), 1
    while stride < count:
        rest = count // stride
        radix = next(f for f in range(2, rest + 1) if rest % f == 0)
        def moved(turn):
            pairs = []
            for source in range(count):
                digit = source // stride % radix
                pairs.append((source, source + ((digit + turn) % radix - digit) * stride))
            return lax.ppermute(x, axis, pairs)
        x = x + sum([moved(turn) for turn in range(1, radix)])
        stride = stride * radix
    return x


def per_device(queries, keys, values, grad_out, query_gain, key_gain, doc_lengths):
    rows = queries.shape[1]
    count = lax.axis_size("ctx")
    assert rows * 2 == WINDOW_SIZE and count % 2 == 0
    here = lax.axis_index("ctx")
    odd = lax.rem(here, 2)
    first = (here * rows).astype(jnp.int32)
    q, k, v, go = queries[0], keys[0], values[0], grad_out[0]
    q_gain, k_gain = query_gain[None], key_gain[None]

    ahead = [(i, (i + 2) % count) for i in range(count)]
    behind = [(i, (i - 2) % count) for i in range(count)]
    follow = [(i, (i + 1) % count) for i in range(count)]
    lead = [(i, (i - 1) % count) for i in range(count)]
    swap = [(i, i ^ 1) for i in range(count)]

    wide, slim, gain, per = specs(rows)
    pair = GROUP * rows
    keys = WINDOW_SIZE + rows
    heads = KEY_VALUE_HEADS
    kv_shape = (rows, heads * HEAD_SIZE)
    tall = pl.BlockSpec((WINDOW_SIZE, UNROLL * HEAD_SIZE), lambda g, *_: (0, g))
    window = pl.BlockSpec((WINDOW_SIZE, rows), lambda g, *_: (0, 0))

    k2 = lax.ppermute(k, "ctx", ahead)
    qn, kn0, s0, dp0, go_t, bias = call(
        prepare_kernel, "prepare", [wide, slim, slim, wide, gain, gain],
        [
            (per(pair, HEAD_SIZE), (heads, pair, HEAD_SIZE), BF16),
            (slim, kv_shape, BF16),
            (per(rows, pair), (heads, rows, pair), F32),
            (per(rows, pair), (heads, rows, pair), F32),
            (per(HEAD_SIZE, pair), (heads, HEAD_SIZE, pair), BF16),
            (window, (WINDOW_SIZE, rows), F32),
        ],
        (q, k, v, go, q_gain, k_gain), (first[None], doc_lengths), [pltpu.VMEM((rows, rows), F32)],
    )
    late_v = lax.optimization_barrier((v, qn))[0]
    v2 = lax.ppermute(late_v, "ctx", ahead)
    v1 = lax.ppermute(late_v, "ctx", follow)
    k1 = lax.ppermute(jnp.where(odd == 1, k2, k), "ctx", swap)

    knx, p, g1v, g2v = call(
        weigh_kernel, "weigh",
        [per(pair, HEAD_SIZE), per(rows, pair), window, slim, slim, wide, gain],
        [
            (tall, (WINDOW_SIZE, heads * HEAD_SIZE), BF16),
            (per(keys, pair), (heads, keys, pair), F32),
            (slim, kv_shape, BF16),
            (slim, kv_shape, BF16),
        ],
        (qn, s0, bias, k1, k2, go, k_gain),
    )
    av = lax.ppermute(g1v, "ctx", lead)
    bv = lax.ppermute(g2v, "ctx", behind)

    ds, g1k, g2k = call(
        score_kernel, "score",
        [per(keys, pair), slim, slim, slim, wide, per(HEAD_SIZE, pair), per(rows, pair), per(pair, HEAD_SIZE)],
        [(per(keys, pair), (heads, keys, pair), BF16), (slim, kv_shape, BF16), (slim, kv_shape, BF16)],
        (p, v, v1, v2, go, go_t, dp0, qn),
    )
    ak = lax.ppermute(g1k, "ctx", swap)
    dq, dk_own, dv_own, gains = call(
        rest_kernel, "rest",
        [wide, per(pair, HEAD_SIZE), tall, slim, per(keys, pair), per(rows, pair, WINDOW_SIZE // rows), wide, gain, gain],
        [
            (wide, q.shape, BF16),
            (slim, kv_shape, F32),
            (slim, kv_shape, F32),
            (pl.BlockSpec((8, HEAD_SIZE), lambda g, *_: (0, 0)), (8, HEAD_SIZE), F32),
        ],
        (q, qn, knx, kn0, ds, p, go, q_gain, k_gain),
    )
    keep = (odd == 1).astype(F32)
    bk = lax.ppermute((g2k.astype(F32) + ak.astype(F32) * keep).astype(BF16), "ctx", behind)
    gains = sum_over(sum_over(gains, "ctx"), "dp")

    dv = call(value_kernel, "value", [slim] * 3, [(slim, kv_shape, BF16)], (dv_own, av, bv))[0]
    dk = call(
        key_kernel, "key", [slim] * 4 + [gain], [(slim, kv_shape, BF16)],
        (k, dk_own, ak, bk, k_gain), (odd.astype(jnp.int32)[None],),
    )[0]
    return (dq[None], dk[None], dv[None], gains[0], gains[1])


def solution(mesh):
    in_specs = (
        P("dp", "ctx", None),
        P("dp", "ctx", None),
        P("dp", "ctx", None),
        P("dp", "ctx", None),
        P(),
        P(),
        P("dp", None),
    )
    out_specs = (P("dp", "ctx", None), P("dp", "ctx", None), P("dp", "ctx", None), P(), P())
    return jax.shard_map(
        per_device, mesh=mesh, in_specs=in_specs, out_specs=out_specs, check_vma=False
    )
```

```python
import jax
import jax.numpy as jnp
from jax import lax
from jax.experimental import pallas as pl
from jax.experimental.pallas import tpu as pltpu
from jax.sharding import PartitionSpec as P


QUERY_HEADS = 16
KEY_VALUE_HEADS = 8
HEAD_SIZE = 128
WINDOW_SIZE = 256
GROUP = QUERY_HEADS // KEY_VALUE_HEADS

norm_epsilon = 1e-06
score_scale = 168.0 ** (-0.5)
MASKED = -1e30
LOG2E = 1.4426950408889634
VMEM_LIMIT = 16 << 20


F32 = jnp.float32
BF16 = jnp.bfloat16


def dot(a, b, ca, cb):
    return lax.dot_general(a, b, (((ca,), (cb,)), ((), ())), preferred_element_type=F32)


def inverse_rms(x):
    return lax.rsqrt(jnp.mean(x * x, axis=-1, keepdims=True) + norm_epsilon)


def document_of(lengths_ref, positions):
    index = jnp.zeros(positions.shape, jnp.int32)
    end = jnp.int32(0)
    for doc in range(lengths_ref.shape[1]):
        end = end + lengths_ref[0, doc]
        index = index + (positions >= end).astype(jnp.int32)
    return index


def mask_bias(lengths_ref, first, keys, rows):
    key_pos = first - WINDOW_SIZE + lax.broadcasted_iota(jnp.int32, (keys, 1), 0)
    query_pos = first + lax.broadcasted_iota(jnp.int32, (1, rows), 1)
    key_doc = jnp.where(key_pos >= 0, document_of(lengths_ref, key_pos), -1)
    query_doc = document_of(lengths_ref, query_pos)
    gap = query_pos - key_pos
    allowed = (key_doc == query_doc) & (gap >= 0) & (gap < WINDOW_SIZE)
    return jnp.where(allowed, 0.0, MASKED).astype(F32)


def stacked(ref, u):
    parts = [ref[:, (u * GROUP + i) * HEAD_SIZE:(u * GROUP + i + 1) * HEAD_SIZE] for i in range(GROUP)]
    return jnp.concatenate(parts, axis=0)


def columns(u):
    return slice(u * HEAD_SIZE, (u + 1) * HEAD_SIZE)


def prepare_kernel(first_ref, lengths_ref, q_ref, k_ref, v_ref, go_ref, qg_ref, kg_ref,
                   q2_ref, qn_ref, kn_ref, s_ref, dp_ref, go2_ref, got_ref, v0_ref, bias_ref):
    rows = q_ref.shape[0]

    bias = mask_bias(lengths_ref, first_ref[0], WINDOW_SIZE + rows, rows)
    bias_ref[...] = bias[:WINDOW_SIZE]
    bias = jnp.concatenate([bias[WINDOW_SIZE:]] * GROUP, axis=1)
    for u in range(KEY_VALUE_HEADS):
        raw = stacked(q_ref, u)
        q2_ref[u] = raw
        q = raw.astype(F32)
        go = stacked(go_ref, u)
        go2_ref[u] = go
        v0_ref[:, columns(u)] = v_ref[:, columns(u)]
        qn = (q * inverse_rms(q) * qg_ref[...]).astype(BF16)
        k = k_ref[:, columns(u)].astype(F32)
        kn = (k * inverse_rms(k) * kg_ref[...]).astype(BF16)
        qn_ref[u] = qn
        kn_ref[:, columns(u)] = kn
        s_ref[u] = dot(kn, qn, 1, 1) * (score_scale * LOG2E) + bias
        dp_ref[u] = dot(v_ref[:, columns(u)], go, 1, 1)
        got_ref[u] = jnp.transpose(go)


def weigh_kernel(qn_ref, kn0_ref, s_ref, bias_ref, k1_ref, k2_ref, go_ref, kg_ref, kn_ref, p_ref, g1v_ref, g2v_ref):
    rows = kn0_ref.shape[0]
    bias = jnp.concatenate([bias_ref[...]] * GROUP, axis=1)
    kn_ref[WINDOW_SIZE:, :] = kn0_ref[...]
    for u in range(KEY_VALUE_HEADS):
        k = jnp.concatenate([k2_ref[:, columns(u)], k1_ref[:, columns(u)]], axis=0).astype(F32)
        kn = (k * inverse_rms(k) * kg_ref[...]).astype(BF16)
        kn_ref[:WINDOW_SIZE, columns(u)] = kn
        s = dot(kn, qn_ref[u], 1, 1) * (score_scale * LOG2E) + bias
        s0 = s_ref[u]
        top = jnp.maximum(jnp.max(s, axis=0, keepdims=True), jnp.max(s0, axis=0, keepdims=True))
        e, e0 = jnp.exp2(s - top), jnp.exp2(s0 - top)
        inv = 1.0 / (jnp.sum(e, axis=0, keepdims=True) + jnp.sum(e0, axis=0, keepdims=True))
        p = e * inv
        p_ref[u, :WINDOW_SIZE] = p
        p_ref[u, WINDOW_SIZE:] = e0 * inv
        g = dot(p.astype(BF16), go_ref[u], 1, 0).astype(BF16)
        g2v_ref[:, columns(u)] = g[:rows]
        g1v_ref[:, columns(u)] = g[rows:]


def score_kernel(p_ref, v0_ref, v1_ref, v2_ref, go_ref, got_ref, dp_ref, q_ref, qn_ref, kn_ref, qg_ref, kg_ref,
                 g1k_ref, g2k_ref, dq_ref, dk_ref, dv_ref, gains_ref):
    rows = v0_ref.shape[0]
    q_part = jnp.zeros((1, HEAD_SIZE), F32)
    k_part = jnp.zeros((1, HEAD_SIZE), F32)
    for u in range(KEY_VALUE_HEADS):
        v = jnp.concatenate([v2_ref[:, columns(u)], v1_ref[:, columns(u)]], axis=0)
        go, qn = go_ref[u], qn_ref[u]
        p, p0 = p_ref[u, :WINDOW_SIZE], p_ref[u, WINDOW_SIZE:]
        p0_low = p0.astype(BF16)
        attended = dot(v, p.astype(BF16), 0, 0) + dot(v0_ref[:, columns(u)], p0_low, 0, 0)
        attended = attended.astype(BF16).astype(F32)
        delta = jnp.sum(got_ref[u].astype(F32) * attended, axis=0, keepdims=True)
        ds = (p * (dot(v, go, 1, 1) - delta)).astype(BF16)
        ds0 = (p0 * (dp_ref[u] - delta)).astype(BF16)
        g = (dot(ds, qn, 1, 0) * score_scale).astype(BF16)
        g2k_ref[:, columns(u)] = g[:rows]
        g1k_ref[:, columns(u)] = g[rows:]
        kn = kn_ref[:, columns(u)]
        dqn = dot(jnp.concatenate([ds, ds0], axis=0), kn, 0, 0) * score_scale
        dk_ref[:, columns(u)] = dot(ds0, qn, 1, 0) * score_scale
        dv_ref[:, columns(u)] = dot(p0_low, go, 1, 0)
        q = q_ref[u].astype(F32)
        q_inv = inverse_rms(q)
        q_hat = q * q_inv
        q_part = q_part + jnp.sum(dqn * q_hat, axis=0, keepdims=True)
        k_part = k_part + jnp.sum(dqn * qn.astype(F32), axis=0, keepdims=True)
        t = dqn * qg_ref[...]
        dq = (q_inv * (t - q_hat * jnp.mean(t * q_hat, axis=-1, keepdims=True))).astype(BF16)
        for i in range(GROUP):
            dq_ref[:, columns(u * GROUP + i)] = dq[i * rows:(i + 1) * rows]
    gains_ref[...] = jnp.zeros_like(gains_ref)
    gains_ref[0:1, :] = q_part
    gains_ref[1:2, :] = k_part / kg_ref[...]


def value_kernel(dv_ref, a_ref, b_ref, out_ref):
    out_ref[...] = (dv_ref[...] + a_ref[...].astype(F32) + b_ref[...].astype(F32)).astype(BF16)


def key_kernel(odd_ref, k_ref, dk_ref, a_ref, b_ref, kg_ref, out_ref):
    keep = (odd_ref[0] == 0).astype(F32)
    for h in range(k_ref.shape[1] // HEAD_SIZE):
        total = dk_ref[:, columns(h)] + a_ref[:, columns(h)].astype(F32) * keep + b_ref[:, columns(h)].astype(F32)
        k = k_ref[:, columns(h)].astype(F32)
        inv = inverse_rms(k)
        k_hat = k * inv
        t = total * kg_ref[...]
        out_ref[:, columns(h)] = (inv * (t - k_hat * jnp.mean(t * k_hat, axis=-1, keepdims=True))).astype(BF16)


def call(kernel, outs, args, scalars=()):
    vmem = pl.BlockSpec(memory_space=pltpu.VMEM)
    return pl.pallas_call(
        kernel,
        in_specs=[pl.BlockSpec(memory_space=pltpu.SMEM)] * len(scalars) + [vmem] * len(args),
        out_specs=[vmem] * len(outs),
        out_shape=outs,
        compiler_params=pltpu.CompilerParams(vmem_limit_bytes=VMEM_LIMIT),
    )(*scalars, *args)


def near(*arrays):
    return tuple(pltpu.with_memory_space_constraint(array, pltpu.VMEM) for array in arrays)


def far(*arrays):
    return tuple(pltpu.with_memory_space_constraint(array, pltpu.HBM) for array in arrays)


def sum_over(x, axis):
    count, stride = lax.axis_size(axis), 1
    while stride < count:
        rest = count // stride
        radix = next(f for f in range(2, rest + 1) if rest % f == 0)

        def moved(turn):
            pairs = []
            for source in range(count):
                digit = source // stride % radix
                pairs.append((source, source + ((digit + turn) % radix - digit) * stride))
            return lax.ppermute(x, axis, pairs)

        parts = [moved(turn) for turn in range(1, radix)]
        x = x + sum(parts)
        stride = stride * radix
    return x


def per_device(queries, keys, values, grad_out, query_gain, key_gain, doc_lengths):
    rows = queries.shape[1]
    count = lax.axis_size("ctx")
    assert rows * 2 == WINDOW_SIZE and count % 2 == 0
    here = lax.axis_index("ctx")
    odd = lax.rem(here, 2)
    first = (here * rows).astype(jnp.int32)
    q, k, v, go = queries[0], keys[0], values[0], grad_out[0]
    q_gain, k_gain = query_gain[None], key_gain[None]

    ahead = [(i, (i + 2) % count) for i in range(count)]
    behind = [(i, (i - 2) % count) for i in range(count)]
    follow = [(i, (i + 1) % count) for i in range(count)]
    lead = [(i, (i - 1) % count) for i in range(count)]
    swap = [(i, i ^ 1) for i in range(count)]

    pair, keys, heads = GROUP * rows, WINDOW_SIZE + rows, KEY_VALUE_HEADS
    flat = (rows, heads * HEAD_SIZE)
    tie = lax.optimization_barrier

    held, away = pltpu.VMEM, jax.ShapeDtypeStruct
    k2 = lax.ppermute(k, "ctx", ahead)
    q2, qn, kn0, s0, dp0, go2, go_t, v0, bias = call(
        prepare_kernel,
        [
            held((heads, pair, HEAD_SIZE), BF16), held((heads, pair, HEAD_SIZE), BF16), held(flat, BF16),
            held((heads, rows, pair), F32), held((heads, rows, pair), F32),
            held((heads, pair, HEAD_SIZE), BF16), held((heads, HEAD_SIZE, pair), BF16),
            held(flat, BF16), held((WINDOW_SIZE, rows), F32),
        ],
        far(q, k, v, go, q_gain, k_gain), (first[None],) + far(doc_lengths),
    )
    turned = jnp.where(odd == 1, k2, k)
    k1 = lax.ppermute(turned, "ctx", swap)
    late_v, _ = tie((v, turned))
    v2 = lax.ppermute(late_v, "ctx", ahead)
    v1 = lax.ppermute(late_v, "ctx", follow)

    kn, p, g1v, g2v = call(
        weigh_kernel,
        [
            held((keys, heads * HEAD_SIZE), BF16), held((heads, keys, pair), F32),
            held(flat, BF16), held(flat, BF16),
        ],
        near(qn, kn0, s0, bias, k1, k2, go2) + far(k_gain),
    )
    av = lax.ppermute(g1v, "ctx", lead)
    bv = lax.ppermute(g2v, "ctx", behind)

    g1k, g2k, dq, dk_own, dv_own, gains = call(
        score_kernel,
        [
            held(flat, BF16), held(flat, BF16), away(q.shape, BF16),
            held(flat, F32), held(flat, F32), held((8, HEAD_SIZE), F32),
        ],
        near(p, v0, v1, v2, go2, go_t, dp0, q2, qn, kn) + far(q_gain, k_gain),
    )
    ak = lax.ppermute(g1k, "ctx", swap)
    keep = (odd == 1).astype(F32)
    joined = (g2k.astype(F32) + ak.astype(F32) * keep).astype(BF16)
    bk = lax.ppermute(joined, "ctx", behind)
    gains = sum_over(sum_over(gains, "dp"), "ctx")

    dv = call(value_kernel, [away(flat, BF16)], near(dv_own, av, bv))[0]
    dk = call(
        key_kernel, [away(flat, BF16)],
        far(k) + near(dk_own, ak, bk) + far(k_gain), (odd.astype(jnp.int32)[None],),
    )[0]
    return (dq[None], dk[None], dv[None], gains[0], gains[1])


def solution(mesh):
    in_specs = (
        P("dp", "ctx", None),
        P("dp", "ctx", None),
        P("dp", "ctx", None),
        P("dp", "ctx", None),
        P(),
        P(),
        P("dp", None),
    )
    out_specs = (P("dp", "ctx", None), P("dp", "ctx", None), P("dp", "ctx", None), P(), P())
    return jax.shard_map(
        per_device, mesh=mesh, in_specs=in_specs, out_specs=out_specs, check_vma=False
    )
```

```python
import jax
import jax.numpy as jnp
from jax import lax
from jax.experimental import pallas as pl
from jax.experimental.pallas import tpu as pltpu
from jax.sharding import PartitionSpec as P


QUERY_HEADS = 16
KEY_VALUE_HEADS = 8
HEAD_SIZE = 128
WINDOW_SIZE = 256
GROUP = QUERY_HEADS // KEY_VALUE_HEADS

norm_epsilon = 1e-06
score_scale = 168.0 ** (-0.5)
MASKED = -1e30
LOG2E = 1.4426950408889634
VMEM_LIMIT = 16 << 20


F32 = jnp.float32
BF16 = jnp.bfloat16


def dot(a, b, ca, cb):
    return lax.dot_general(a, b, (((ca,), (cb,)), ((), ())), preferred_element_type=F32)


def inverse_rms(x):
    return lax.rsqrt(jnp.mean(x * x, axis=-1, keepdims=True) + norm_epsilon)


def document_of(lengths_ref, positions):
    index = jnp.zeros(positions.shape, jnp.int32)
    end = jnp.int32(0)
    for doc in range(lengths_ref.shape[1]):
        end = end + lengths_ref[0, doc]
        index = index + (positions >= end).astype(jnp.int32)
    return index


def mask_bias(lengths_ref, first, keys, rows):
    key_pos = first - WINDOW_SIZE + lax.broadcasted_iota(jnp.int32, (keys, 1), 0)
    query_pos = first + lax.broadcasted_iota(jnp.int32, (1, rows), 1)
    key_doc = jnp.where(key_pos >= 0, document_of(lengths_ref, key_pos), -1)
    query_doc = document_of(lengths_ref, query_pos)
    gap = query_pos - key_pos
    allowed = (key_doc == query_doc) & (gap >= 0) & (gap < WINDOW_SIZE)
    return jnp.where(allowed, 0.0, MASKED).astype(F32)


def stacked(ref, u):
    parts = [ref[:, (u * GROUP + i) * HEAD_SIZE:(u * GROUP + i + 1) * HEAD_SIZE] for i in range(GROUP)]
    return jnp.concatenate(parts, axis=0)


def columns(u):
    return slice(u * HEAD_SIZE, (u + 1) * HEAD_SIZE)


def prepare_kernel(first_ref, lengths_ref, q_ref, k_ref, v_ref, go_ref, qg_ref, kg_ref,
                   q2_ref, qn_ref, kn_ref, s_ref, dp_ref, go2_ref, got_ref, v0_ref, bias_ref, k0_ref, kh_ref, ki_ref, qgo_ref, kgo_ref):
    qgo_ref[...] = qg_ref[...]
    kgo_ref[...] = kg_ref[...]
    rows = q_ref.shape[0]

    bias = mask_bias(lengths_ref, first_ref[0], WINDOW_SIZE + rows, rows)
    bias_ref[...] = bias[:WINDOW_SIZE]
    bias = jnp.concatenate([bias[WINDOW_SIZE:]] * GROUP, axis=1)
    for u in range(KEY_VALUE_HEADS):
        raw = stacked(q_ref, u)
        q2_ref[u] = raw
        q = raw.astype(F32)
        go = stacked(go_ref, u)
        go2_ref[u] = go
        v0_ref[:, columns(u)] = v_ref[:, columns(u)]
        qn = (q * inverse_rms(q) * qg_ref[...]).astype(BF16)
        raw_k = k_ref[:, columns(u)]
        k0_ref[:, columns(u)] = raw_k
        k = raw_k.astype(F32)
        k_inv = inverse_rms(k)
        k_hat = k * k_inv
        kh_ref[:, columns(u)] = k_hat
        ki_ref[:, columns(u)] = jnp.broadcast_to(k_inv, k.shape)
        kn = (k_hat * kg_ref[...]).astype(BF16)
        qn_ref[u] = qn
        kn_ref[:, columns(u)] = kn
        s_ref[u] = dot(kn, qn, 1, 1) * (score_scale * LOG2E) + bias
        dp_ref[u] = dot(v_ref[:, columns(u)], go, 1, 1)
        got_ref[u] = jnp.transpose(go)


def weigh_kernel(qn_ref, kn0_ref, s_ref, bias_ref, k1_ref, k2_ref, go_ref, kg_ref, kn_ref, p_ref, g1v_ref, g2v_ref):
    rows = kn0_ref.shape[0]
    bias = jnp.concatenate([bias_ref[...]] * GROUP, axis=1)
    kn_ref[WINDOW_SIZE:, :] = kn0_ref[...]
    for u in range(KEY_VALUE_HEADS):
        k = jnp.concatenate([k2_ref[:, columns(u)], k1_ref[:, columns(u)]], axis=0).astype(F32)
        kn = (k * inverse_rms(k) * kg_ref[...]).astype(BF16)
        kn_ref[:WINDOW_SIZE, columns(u)] = kn
        s = dot(kn, qn_ref[u], 1, 1) * (score_scale * LOG2E) + bias
        s0 = s_ref[u]
        top = jnp.maximum(jnp.max(s, axis=0, keepdims=True), jnp.max(s0, axis=0, keepdims=True))
        e, e0 = jnp.exp2(s - top), jnp.exp2(s0 - top)
        inv = 1.0 / (jnp.sum(e, axis=0, keepdims=True) + jnp.sum(e0, axis=0, keepdims=True))
        p = e * inv
        p_ref[u, :WINDOW_SIZE] = p
        p_ref[u, WINDOW_SIZE:] = e0 * inv
        g = dot(p.astype(BF16), go_ref[u], 1, 0).astype(BF16)
        g2v_ref[:, columns(u)] = g[:rows]
        g1v_ref[:, columns(u)] = g[rows:]


def score_kernel(p_ref, v0_ref, v1_ref, v2_ref, go_ref, got_ref, dp_ref, q_ref, qn_ref, kn_ref, qg_ref, kg_ref,
                 g1k_ref, g2k_ref, dq_ref, dk_ref, dv_ref, gains_ref):
    rows = v0_ref.shape[0]
    q_part = jnp.zeros((1, HEAD_SIZE), F32)
    k_part = jnp.zeros((1, HEAD_SIZE), F32)
    for u in range(KEY_VALUE_HEADS):
        v = jnp.concatenate([v2_ref[:, columns(u)], v1_ref[:, columns(u)]], axis=0)
        go, qn = go_ref[u], qn_ref[u]
        p, p0 = p_ref[u, :WINDOW_SIZE], p_ref[u, WINDOW_SIZE:]
        p0_low = p0.astype(BF16)
        attended = dot(v, p.astype(BF16), 0, 0) + dot(v0_ref[:, columns(u)], p0_low, 0, 0)
        attended = attended.astype(BF16).astype(F32)
        delta = jnp.sum(got_ref[u].astype(F32) * attended, axis=0, keepdims=True)
        ds = (p * (dot(v, go, 1, 1) - delta)).astype(BF16)
        ds0 = (p0 * (dp_ref[u] - delta)).astype(BF16)
        g = (dot(ds, qn, 1, 0) * score_scale).astype(BF16)
        g2k_ref[:, columns(u)] = g[:rows]
        g1k_ref[:, columns(u)] = g[rows:]
        kn = kn_ref[:, columns(u)]
        dqn = dot(jnp.concatenate([ds, ds0], axis=0), kn, 0, 0) * score_scale
        dk_ref[:, columns(u)] = dot(ds0, qn, 1, 0) * score_scale
        dv_ref[:, columns(u)] = dot(p0_low, go, 1, 0)
        q = q_ref[u].astype(F32)
        q_inv = inverse_rms(q)
        q_hat = q * q_inv
        q_part = q_part + jnp.sum(dqn * q_hat, axis=0, keepdims=True)
        k_part = k_part + jnp.sum(dqn * qn.astype(F32), axis=0, keepdims=True)
        t = dqn * qg_ref[...]
        dq = (q_inv * (t - q_hat * jnp.mean(t * q_hat, axis=-1, keepdims=True))).astype(BF16)
        for i in range(GROUP):
            dq_ref[:, columns(u * GROUP + i)] = dq[i * rows:(i + 1) * rows]
    parts = jnp.concatenate([q_part, k_part / kg_ref[...]], axis=0)
    gains_ref[...] = jnp.broadcast_to(parts[None], gains_ref.shape)


def value_kernel(dv_ref, a_ref, b_ref, out_ref):
    out_ref[...] = (dv_ref[...] + a_ref[...].astype(F32) + b_ref[...].astype(F32)).astype(BF16)


def key_kernel(odd_ref, kh_ref, ki_ref, dk_ref, a_ref, b_ref, kg_ref, out_ref):
    keep = (odd_ref[0] == 0).astype(F32)
    for u in range(KEY_VALUE_HEADS):
        total = dk_ref[:, columns(u)] + a_ref[:, columns(u)].astype(F32) * keep + b_ref[:, columns(u)].astype(F32)
        k_hat = kh_ref[:, columns(u)]
        t = total * kg_ref[...]
        dk = ki_ref[:, columns(u)] * (t - k_hat * jnp.mean(t * k_hat, axis=-1, keepdims=True))
        out_ref[:, columns(u)] = dk.astype(BF16)


def call(kernel, outs, args, scalars=()):
    vmem = pl.BlockSpec(memory_space=pltpu.VMEM)
    return pl.pallas_call(
        kernel,
        in_specs=[pl.BlockSpec(memory_space=pltpu.SMEM)] * len(scalars) + [vmem] * len(args),
        out_specs=[vmem] * len(outs),
        out_shape=outs,
        compiler_params=pltpu.CompilerParams(vmem_limit_bytes=VMEM_LIMIT),
    )(*scalars, *args)


def near(*arrays):
    return tuple(pltpu.with_memory_space_constraint(array, pltpu.VMEM) for array in arrays)


def far(*arrays):
    return tuple(pltpu.with_memory_space_constraint(array, pltpu.HBM) for array in arrays)


def per_device(queries, keys, values, grad_out, query_gain, key_gain, doc_lengths):
    rows = queries.shape[1]
    count = lax.axis_size("ctx")
    assert rows * 2 == WINDOW_SIZE and count % 2 == 0
    here = lax.axis_index("ctx")
    odd = lax.rem(here, 2)
    first = (here * rows).astype(jnp.int32)
    q, k, v, go = queries[0], keys[0], values[0], grad_out[0]
    q_gain, k_gain = query_gain[None], key_gain[None]

    ahead = [(i, (i + 2) % count) for i in range(count)]
    behind = [(i, (i - 2) % count) for i in range(count)]
    follow = [(i, (i + 1) % count) for i in range(count)]
    lead = [(i, (i - 1) % count) for i in range(count)]
    swap = [(i, i ^ 1) for i in range(count)]

    pair, keys, heads = GROUP * rows, WINDOW_SIZE + rows, KEY_VALUE_HEADS
    flat = (rows, heads * HEAD_SIZE)
    devices = count * lax.axis_size("dp")
    tie = lax.optimization_barrier

    held, away = pltpu.VMEM, jax.ShapeDtypeStruct
    k2 = lax.ppermute(k, "ctx", ahead)
    q2, qn, kn0, s0, dp0, go2, go_t, v0, bias, k0, k_hat, k_inv, qg, kg = call(
        prepare_kernel,
        [
            held((heads, pair, HEAD_SIZE), BF16), held((heads, pair, HEAD_SIZE), BF16), held(flat, BF16),
            held((heads, rows, pair), F32), held((heads, rows, pair), F32),
            held((heads, pair, HEAD_SIZE), BF16), held((heads, HEAD_SIZE, pair), BF16),
            held(flat, BF16), held((WINDOW_SIZE, rows), F32), held(flat, BF16), held(flat, F32), held(flat, F32),
            held((1, HEAD_SIZE), F32), held((1, HEAD_SIZE), F32),
        ],
        far(q, k, v, go, q_gain, k_gain), (first[None],) + far(doc_lengths),
    )
    turned = jnp.where(odd == 1, k2, k0)
    k1 = lax.ppermute(turned, "ctx", swap)
    late_v, _ = tie((v, turned))
    v2 = lax.ppermute(late_v, "ctx", ahead)
    v1 = lax.ppermute(late_v, "ctx", follow)

    kn, p, g1v, g2v = call(
        weigh_kernel,
        [
            held((keys, heads * HEAD_SIZE), BF16), held((heads, keys, pair), F32),
            held(flat, BF16), held(flat, BF16),
        ],
        near(qn, kn0, s0, bias, k1, k2, go2, kg),
    )
    av = lax.ppermute(g1v, "ctx", lead)
    bv = lax.ppermute(g2v, "ctx", behind)

    g1k, g2k, dq, dk_own, dv_own, gains = call(
        score_kernel,
        [
            held(flat, BF16), held(flat, BF16), away(q.shape, BF16),
            held(flat, F32), held(flat, F32), held((devices, 2, HEAD_SIZE), F32),
        ],
        near(p, v0, v1, v2, go2, go_t, dp0, q2, qn, kn, qg, kg),
    )
    ak = lax.ppermute(g1k, "ctx", swap)
    keep = (odd == 1).astype(F32)
    joined = (g2k.astype(F32) + ak.astype(F32) * keep).astype(BF16)
    bk = lax.ppermute(joined, "ctx", behind)
    spread = lax.all_to_all(gains, ("ctx", "dp"), 0, 0)
    gains = jnp.sum(spread, axis=0)

    dv = call(value_kernel, [away(flat, BF16)], near(dv_own, av, bv))[0]
    dk = call(
        key_kernel, [away(flat, BF16)],
        near(k_hat, k_inv, dk_own, ak, bk, kg), (odd.astype(jnp.int32)[None],),
    )[0]
    return (dq[None], dk[None], dv[None], gains[0], gains[1])


def solution(mesh):
    in_specs = (
        P("dp", "ctx", None),
        P("dp", "ctx", None),
        P("dp", "ctx", None),
        P("dp", "ctx", None),
        P(),
        P(),
        P("dp", None),
    )
    out_specs = (P("dp", "ctx", None), P("dp", "ctx", None), P("dp", "ctx", None), P(), P())
    return jax.shard_map(
        per_device, mesh=mesh, in_specs=in_specs, out_specs=out_specs, check_vma=False
    )
```

```python
import jax
import jax.numpy as jnp
from jax import lax
from jax.experimental import pallas as pl
from jax.experimental.pallas import tpu as pltpu
from jax.sharding import PartitionSpec as P


QUERY_HEADS = 16
KEY_VALUE_HEADS = 8
HEAD_SIZE = 128
WINDOW_SIZE = 256
GROUP = QUERY_HEADS // KEY_VALUE_HEADS

norm_epsilon = 1e-06
score_scale = 168.0 ** (-0.5)
MASKED = -1e30
LOG2E = 1.4426950408889634
VMEM_LIMIT = 16 << 20


F32 = jnp.float32
BF16 = jnp.bfloat16


def dot(a, b, ca, cb):
    return lax.dot_general(a, b, (((ca,), (cb,)), ((), ())), preferred_element_type=F32)


def inverse_rms(x):
    return lax.rsqrt(jnp.mean(x * x, axis=-1, keepdims=True) + norm_epsilon)


def document_of(lengths_ref, positions):
    index = jnp.zeros(positions.shape, jnp.int32)
    end = jnp.int32(0)
    for doc in range(lengths_ref.shape[1]):
        end = end + lengths_ref[0, doc]
        index = index + (positions >= end).astype(jnp.int32)
    return index


def mask_bias(lengths_ref, first, keys, rows):
    key_pos = first - WINDOW_SIZE + lax.broadcasted_iota(jnp.int32, (keys, 1), 0)
    query_pos = first + lax.broadcasted_iota(jnp.int32, (1, rows), 1)
    key_doc = jnp.where(key_pos >= 0, document_of(lengths_ref, key_pos), -1)
    query_doc = document_of(lengths_ref, query_pos)
    gap = query_pos - key_pos
    allowed = (key_doc == query_doc) & (gap >= 0) & (gap < WINDOW_SIZE)
    return jnp.where(allowed, 0.0, MASKED).astype(F32)


def stacked(ref, u):
    parts = [ref[:, (u * GROUP + i) * HEAD_SIZE:(u * GROUP + i + 1) * HEAD_SIZE] for i in range(GROUP)]
    return jnp.concatenate(parts, axis=0)


def columns(u):
    return slice(u * HEAD_SIZE, (u + 1) * HEAD_SIZE)


def prepare_kernel(first_ref, lengths_ref, q_ref, k_ref, v_ref, go_ref, qg_ref, kg_ref,
                   qh_ref, qn_ref, kn_ref, s_ref, dp_ref, go2_ref, got_ref, v0_ref, bias_ref, k0_ref, qgo_ref, kgo_ref):
    qgo_ref[...] = qg_ref[...]
    kgo_ref[...] = kg_ref[...]
    rows = q_ref.shape[0]

    bias = mask_bias(lengths_ref, first_ref[0], WINDOW_SIZE + rows, rows)
    bias_ref[...] = bias[:WINDOW_SIZE]
    bias = jnp.concatenate([bias[WINDOW_SIZE:]] * GROUP, axis=1)
    for u in range(KEY_VALUE_HEADS):
        raw = stacked(q_ref, u)
        q = raw.astype(F32)
        q_inv = inverse_rms(q)
        q_hat = q * q_inv
        qh_ref[u] = q_hat
        go = stacked(go_ref, u)
        go2_ref[u] = go
        v0_ref[:, columns(u)] = v_ref[:, columns(u)]
        qn = (q_hat * qg_ref[...]).astype(BF16)
        raw_k = k_ref[:, columns(u)]
        k0_ref[:, columns(u)] = raw_k
        k = raw_k.astype(F32)
        kn = (k * inverse_rms(k) * kg_ref[...]).astype(BF16)
        qn_ref[u] = qn
        kn_ref[:, columns(u)] = kn
        s_ref[u] = dot(kn, qn, 1, 1) * (score_scale * LOG2E) + bias
        dp_ref[u] = dot(v_ref[:, columns(u)], go, 1, 1)
        got_ref[u] = jnp.transpose(go)


def early_kernel(qn_ref, s_ref, bias_ref, k2_ref, kg_ref, kn_ref, e_ref, top_ref, sum_ref):
    rows = k2_ref.shape[0]
    bias = jnp.concatenate([bias_ref[:rows]] * GROUP, axis=1)
    for u in range(KEY_VALUE_HEADS):
        k = k2_ref[:, columns(u)].astype(F32)
        kn = (k * inverse_rms(k) * kg_ref[...]).astype(BF16)
        kn_ref[:, columns(u)] = kn
        s2 = dot(kn, qn_ref[u], 1, 1) * (score_scale * LOG2E) + bias
        s0 = s_ref[u]
        top = jnp.maximum(jnp.max(s2, axis=0, keepdims=True), jnp.max(s0, axis=0, keepdims=True))
        e2, e0 = jnp.exp2(s2 - top), jnp.exp2(s0 - top)
        e_ref[u, :rows] = e2
        e_ref[u, rows:] = e0
        top_ref[u] = top
        sum_ref[u] = jnp.sum(e2, axis=0, keepdims=True) + jnp.sum(e0, axis=0, keepdims=True)


def weigh_kernel(qn_ref, e_ref, top_ref, sum_ref, bias_ref, k1_ref, go_ref, kg_ref, kn_ref, p_ref, low_ref, g1v_ref, g2v_ref):
    rows = k1_ref.shape[0]
    bias = jnp.concatenate([bias_ref[rows:]] * GROUP, axis=1)
    for u in range(KEY_VALUE_HEADS):
        k = k1_ref[:, columns(u)].astype(F32)
        kn = (k * inverse_rms(k) * kg_ref[...]).astype(BF16)
        kn_ref[:, columns(u)] = kn
        s1 = dot(kn, qn_ref[u], 1, 1) * (score_scale * LOG2E) + bias
        top = jnp.maximum(top_ref[u], jnp.max(s1, axis=0, keepdims=True))
        e1 = jnp.exp2(s1 - top)
        fade = jnp.exp2(top_ref[u] - top)
        inv = 1.0 / (sum_ref[u] * fade + jnp.sum(e1, axis=0, keepdims=True))
        fade = fade * inv
        p2 = e_ref[u, :rows] * fade
        p1 = e1 * inv
        p_ref[u, :rows] = p2
        p_ref[u, rows:WINDOW_SIZE] = p1
        p0 = e_ref[u, rows:] * fade
        p_ref[u, WINDOW_SIZE:] = p0
        low_ref[u] = p0.astype(BF16)
        g1v_ref[:, columns(u)] = dot(p1.astype(BF16), go_ref[u], 1, 0).astype(BF16)
        g2v_ref[:, columns(u)] = dot(p2.astype(BF16), go_ref[u], 1, 0).astype(BF16)


def score_kernel(p_ref, low_ref, v0_ref, v1_ref, v2_ref, go_ref, got_ref, dp_ref, qh_ref, qn_ref, kn2_ref, kn1_ref, kn0_ref,
                 kg_ref, g1k_ref, g2k_ref, ds_ref, dqn_ref, gains_ref):
    rows = v0_ref.shape[0]
    q_part = jnp.zeros((1, HEAD_SIZE), F32)
    k_part = jnp.zeros((1, HEAD_SIZE), F32)
    for u in range(KEY_VALUE_HEADS):
        v = jnp.concatenate([v2_ref[:, columns(u)], v1_ref[:, columns(u)]], axis=0)
        qn = qn_ref[u]
        p, p0 = p_ref[u, :WINDOW_SIZE], p_ref[u, WINDOW_SIZE:]
        attended = dot(v, p.astype(BF16), 0, 0) + dot(v0_ref[:, columns(u)], low_ref[u], 0, 0)
        attended = attended.astype(BF16).astype(F32)
        delta = jnp.sum(got_ref[u].astype(F32) * attended, axis=0, keepdims=True)
        ds = (p * (dot(v, go_ref[u], 1, 1) - delta)).astype(BF16)
        ds0 = (p0 * (dp_ref[u] - delta)).astype(BF16)
        ds_ref[u] = ds0
        g = (dot(ds, qn, 1, 0) * score_scale).astype(BF16)
        g2k_ref[:, columns(u)] = g[:rows]
        g1k_ref[:, columns(u)] = g[rows:]
        kn = jnp.concatenate([ref[:, columns(u)] for ref in (kn2_ref, kn1_ref, kn0_ref)], axis=0)
        dqn = dot(jnp.concatenate([ds, ds0], axis=0), kn, 0, 0) * score_scale
        dqn_ref[u] = dqn
        q_part = q_part + jnp.sum(dqn * qh_ref[u], axis=0, keepdims=True)
        k_part = k_part + jnp.sum(dqn * qn.astype(F32), axis=0, keepdims=True)
    parts = jnp.concatenate([q_part, k_part / kg_ref[...]], axis=0)
    gains_ref[...] = jnp.broadcast_to(parts[None], gains_ref.shape)


def rest_kernel(q_ref, go_ref, low_ref, ds_ref, dqn_ref, qg_ref, a_ref, b_ref,
                dq_ref, dk_ref, dv_ref):
    rows = a_ref.shape[0]
    for u in range(KEY_VALUE_HEADS):
        own = dot(low_ref[u], stacked(go_ref, u), 1, 0)
        total = own + a_ref[:, columns(u)].astype(F32) + b_ref[:, columns(u)].astype(F32)
        dv_ref[:, columns(u)] = total.astype(BF16)
        q = stacked(q_ref, u).astype(F32)
        q_inv = inverse_rms(q)
        q_hat = q * q_inv
        dk_ref[:, columns(u)] = dot(ds_ref[u], (q_hat * qg_ref[...]).astype(BF16), 1, 0) * score_scale
        t = dqn_ref[u] * qg_ref[...]
        dq = (q_inv * (t - q_hat * jnp.mean(t * q_hat, axis=-1, keepdims=True))).astype(BF16)
        for i in range(GROUP):
            dq_ref[:, columns(u * GROUP + i)] = dq[i * rows:(i + 1) * rows]


def turn_kernel(odd_ref, own_ref, got_ref, out_ref):
    out_ref[...] = jnp.where(odd_ref[0] == 1, got_ref[...], own_ref[...])


def join_kernel(odd_ref, own_ref, got_ref, out_ref):
    keep = (odd_ref[0] == 1).astype(F32)
    out_ref[...] = (own_ref[...].astype(F32) + got_ref[...].astype(F32) * keep).astype(BF16)


def total_kernel(k_ref, parts_ref, q_out_ref, k_out_ref, kh_ref, ki_ref):
    total = jnp.sum(parts_ref[...], axis=0)
    q_out_ref[...] = total[0:1]
    k_out_ref[...] = total[1:2]
    for u in range(KEY_VALUE_HEADS):
        k = k_ref[:, columns(u)].astype(F32)
        k_inv = inverse_rms(k)
        kh_ref[:, columns(u)] = k * k_inv
        ki_ref[:, columns(u)] = jnp.broadcast_to(k_inv, k.shape)


def key_kernel(odd_ref, kh_ref, ki_ref, dk_ref, a_ref, b_ref, kg_ref, out_ref):
    keep = (odd_ref[0] == 0).astype(F32)
    for u in range(KEY_VALUE_HEADS):
        total = dk_ref[:, columns(u)] + a_ref[:, columns(u)].astype(F32) * keep + b_ref[:, columns(u)].astype(F32)
        k_hat = kh_ref[:, columns(u)]
        t = total * kg_ref[...]
        dk = ki_ref[:, columns(u)] * (t - k_hat * jnp.mean(t * k_hat, axis=-1, keepdims=True))
        out_ref[:, columns(u)] = dk.astype(BF16)


def call(kernel, outs, args, scalars=()):
    vmem = pl.BlockSpec(memory_space=pltpu.VMEM)
    return pl.pallas_call(
        kernel,
        in_specs=[pl.BlockSpec(memory_space=pltpu.SMEM)] * len(scalars) + [vmem] * len(args),
        out_specs=[vmem] * len(outs),
        out_shape=outs,
        compiler_params=pltpu.CompilerParams(vmem_limit_bytes=VMEM_LIMIT),
    )(*scalars, *args)


def near(*arrays):
    return tuple(pltpu.with_memory_space_constraint(array, pltpu.VMEM) for array in arrays)


def far(*arrays):
    return tuple(pltpu.with_memory_space_constraint(array, pltpu.HBM) for array in arrays)


def per_device(queries, keys, values, grad_out, query_gain, key_gain, doc_lengths):
    rows = queries.shape[1]
    count = lax.axis_size("ctx")
    assert rows * 2 == WINDOW_SIZE and count % 2 == 0
    here = lax.axis_index("ctx")
    odd = lax.rem(here, 2)
    first = (here * rows).astype(jnp.int32)
    q, k, v, go = queries[0], keys[0], values[0], grad_out[0]
    q_gain, k_gain = query_gain[None], key_gain[None]

    ahead = [(i, (i + 2) % count) for i in range(count)]
    behind = [(i, (i - 2) % count) for i in range(count)]
    follow = [(i, (i + 1) % count) for i in range(count)]
    lead = [(i, (i - 1) % count) for i in range(count)]
    swap = [(i, i ^ 1) for i in range(count)]

    pair, keys, heads = GROUP * rows, WINDOW_SIZE + rows, KEY_VALUE_HEADS
    flat = (rows, heads * HEAD_SIZE)
    devices = count * lax.axis_size("dp")
    parity = odd.astype(jnp.int32)[None]

    held, away = pltpu.VMEM, jax.ShapeDtypeStruct
    k2 = lax.ppermute(k, "ctx", ahead)
    q_hat, qn, kn0, s0, dp0, go2, go_t, v0, bias, k0, qg, kg = call(
        prepare_kernel,
        [
            held((heads, pair, HEAD_SIZE), F32),
            held((heads, pair, HEAD_SIZE), BF16), held(flat, BF16),
            held((heads, rows, pair), F32), held((heads, rows, pair), F32),
            held((heads, pair, HEAD_SIZE), BF16), held((heads, HEAD_SIZE, pair), BF16),
            held(flat, BF16), held((WINDOW_SIZE, rows), F32), held(flat, BF16),
            held((1, HEAD_SIZE), F32), held((1, HEAD_SIZE), F32),
        ],
        far(q, k, v, go, q_gain, k_gain), (first[None],) + far(doc_lengths),
    )
    turned = call(turn_kernel, [held(flat, BF16)], near(k0, k2), (parity,))[0]
    k1 = lax.ppermute(turned, "ctx", swap)
    v2 = lax.ppermute(v, "ctx", ahead)
    v1 = lax.ppermute(v, "ctx", follow)

    kn2, e, top, norm = call(
        early_kernel,
        [
            held(flat, BF16), held((heads, WINDOW_SIZE, pair), F32),
            held((heads, 1, pair), F32), held((heads, 1, pair), F32),
        ],
        near(qn, s0, bias, k2, kg),
    )
    kn1, p, p_low, g1v, g2v = call(
        weigh_kernel,
        [
            held(flat, BF16), held((heads, keys, pair), F32), held((heads, rows, pair), BF16),
            held(flat, BF16), held(flat, BF16),
        ],
        near(qn, e, top, norm, bias, k1, go2, kg),
    )
    av = lax.ppermute(g1v, "ctx", lead)
    bv = lax.ppermute(g2v, "ctx", behind)

    g1k, g2k, ds0, dqn, gains = call(
        score_kernel,
        [
            held(flat, BF16), held(flat, BF16), held((heads, rows, pair), BF16),
            held((heads, pair, HEAD_SIZE), F32), held((devices, 2, HEAD_SIZE), F32),
        ],
        near(p, p_low, v0, v1, v2, go2, go_t, dp0, q_hat, qn, kn2, kn1, kn0, kg),
    )
    ak = lax.ppermute(g1k, "ctx", swap)
    joined = call(join_kernel, [held(flat, BF16)], near(g2k, ak), (parity,))[0]
    bk = lax.ppermute(joined, "ctx", behind)
    spread = lax.all_to_all(gains, ("ctx", "dp"), 0, 0)
    line = away((1, HEAD_SIZE), F32)
    q_total, k_total, k_hat, k_inv = call(
        total_kernel, [line, line, held(flat, F32), held(flat, F32)], far(k) + near(spread)
    )

    dq, dk_own, dv = call(
        rest_kernel, [away(q.shape, BF16), held(flat, F32), away(flat, BF16)],
        far(q, go) + near(p_low, ds0, dqn, qg) + far(av, bv),
    )
    dk = call(
        key_kernel, [away(flat, BF16)],
        near(k_hat, k_inv, dk_own, ak, bk, kg), (parity,),
    )[0]
    return (dq[None], dk[None], dv[None], q_total[0], k_total[0])


def solution(mesh):
    in_specs = (
        P("dp", "ctx", None),
        P("dp", "ctx", None),
        P("dp", "ctx", None),
        P("dp", "ctx", None),
        P(),
        P(),
        P("dp", None),
    )
    out_specs = (P("dp", "ctx", None), P("dp", "ctx", None), P("dp", "ctx", None), P(), P())
    return jax.shard_map(
        per_device, mesh=mesh, in_specs=in_specs, out_specs=out_specs, check_vma=False
    )
```

```python
import jax
import jax.numpy as jnp
from jax import lax
from jax.experimental import pallas as pl
from jax.experimental.pallas import tpu as pltpu
from jax.sharding import PartitionSpec as P


QUERY_HEADS = 16
KEY_VALUE_HEADS = 8
HEAD_SIZE = 128
WINDOW_SIZE = 256
GROUP = QUERY_HEADS // KEY_VALUE_HEADS

norm_epsilon = 1e-06
score_scale = 168.0 ** (-0.5)
MASKED = -1e30
LOG2E = 1.4426950408889634
VMEM_LIMIT = 16 << 20


F32 = jnp.float32
BF16 = jnp.bfloat16


def dot(a, b, ca, cb):
    return lax.dot_general(a, b, (((ca,), (cb,)), ((), ())), preferred_element_type=F32)


def inverse_rms(x):
    return lax.rsqrt(jnp.mean(x * x, axis=-1, keepdims=True) + norm_epsilon)


def document_of(lengths_ref, positions):
    index = jnp.zeros(positions.shape, jnp.int32)
    end = jnp.int32(0)
    for doc in range(lengths_ref.shape[1]):
        end = end + lengths_ref[0, doc]
        index = index + (positions >= end).astype(jnp.int32)
    return index


def mask_bias(lengths_ref, first, keys, rows):
    key_pos = first - WINDOW_SIZE + lax.broadcasted_iota(jnp.int32, (keys, 1), 0)
    query_pos = first + lax.broadcasted_iota(jnp.int32, (1, rows), 1)
    key_doc = jnp.where(key_pos >= 0, document_of(lengths_ref, key_pos), -1)
    query_doc = document_of(lengths_ref, query_pos)
    gap = query_pos - key_pos
    allowed = (key_doc == query_doc) & (gap >= 0) & (gap < WINDOW_SIZE)
    return jnp.where(allowed, 0.0, MASKED).astype(F32)


def stacked(ref, u):
    parts = [ref[:, (u * GROUP + i) * HEAD_SIZE:(u * GROUP + i + 1) * HEAD_SIZE] for i in range(GROUP)]
    return jnp.concatenate(parts, axis=0)


def columns(u):
    return slice(u * HEAD_SIZE, (u + 1) * HEAD_SIZE)


def prepare_kernel(first_ref, lengths_ref, q_ref, k_ref, v_ref, go_ref, qg_ref, kg_ref,
                   qh_ref, qn_ref, kn_ref, s_ref, dp_ref, go2_ref, got_ref, v0_ref, bias_ref, k0_ref, qgo_ref, kgo_ref):
    qgo_ref[...] = qg_ref[...]
    kgo_ref[...] = kg_ref[...]
    rows = q_ref.shape[0]

    bias = mask_bias(lengths_ref, first_ref[0], WINDOW_SIZE + rows, rows)
    bias_ref[...] = bias[:WINDOW_SIZE]
    bias = jnp.concatenate([bias[WINDOW_SIZE:]] * GROUP, axis=1)
    for u in range(KEY_VALUE_HEADS):
        raw = stacked(q_ref, u)
        q = raw.astype(F32)
        q_inv = inverse_rms(q)
        q_hat = q * q_inv
        qh_ref[u] = q_hat
        go = stacked(go_ref, u)
        go2_ref[u] = go
        v0_ref[:, columns(u)] = v_ref[:, columns(u)]
        qn = (q_hat * qg_ref[...]).astype(BF16)
        raw_k = k_ref[:, columns(u)]
        k0_ref[:, columns(u)] = raw_k
        k = raw_k.astype(F32)
        kn = (k * inverse_rms(k) * kg_ref[...]).astype(BF16)
        qn_ref[u] = qn
        kn_ref[:, columns(u)] = kn
        s_ref[u] = dot(kn, qn, 1, 1) * (score_scale * LOG2E) + bias
        dp_ref[u] = dot(v_ref[:, columns(u)], go, 1, 1)
        got_ref[u] = jnp.transpose(go)


def early_kernel(qn_ref, s_ref, bias_ref, k2_ref, kg_ref, kn_ref, e_ref, top_ref, sum_ref):
    rows = k2_ref.shape[0]
    bias = jnp.concatenate([bias_ref[:rows]] * GROUP, axis=1)
    for u in range(KEY_VALUE_HEADS):
        k = k2_ref[:, columns(u)].astype(F32)
        kn = (k * inverse_rms(k) * kg_ref[...]).astype(BF16)
        kn_ref[:, columns(u)] = kn
        s2 = dot(kn, qn_ref[u], 1, 1) * (score_scale * LOG2E) + bias
        s0 = s_ref[u]
        top = jnp.maximum(jnp.max(s2, axis=0, keepdims=True), jnp.max(s0, axis=0, keepdims=True))
        e2, e0 = jnp.exp2(s2 - top), jnp.exp2(s0 - top)
        e_ref[u, :rows] = e2
        e_ref[u, rows:] = e0
        top_ref[u] = top
        sum_ref[u] = jnp.sum(e2, axis=0, keepdims=True) + jnp.sum(e0, axis=0, keepdims=True)


def weigh_kernel(qn_ref, e_ref, top_ref, sum_ref, bias_ref, k1_ref, go_ref, kg_ref, kn_ref, p_ref, low_ref, g1v_ref, g2v_ref):
    rows = k1_ref.shape[0]
    bias = jnp.concatenate([bias_ref[rows:]] * GROUP, axis=1)
    ready = {}
    for turn in range(KEY_VALUE_HEADS + 2):
        u = turn
        if u < KEY_VALUE_HEADS:
            k = k1_ref[:, columns(u)].astype(F32)
            kn = (k * inverse_rms(k) * kg_ref[...]).astype(BF16)
            kn_ref[:, columns(u)] = kn
            ready[u] = dot(kn, qn_ref[u], 1, 1) * (score_scale * LOG2E) + bias
        u = turn - 2
        if u >= 0:
            s1 = ready.pop(u)
            top = jnp.maximum(top_ref[u], jnp.max(s1, axis=0, keepdims=True))
            e1 = jnp.exp2(s1 - top)
            fade = jnp.exp2(top_ref[u] - top)
            inv = 1.0 / (sum_ref[u] * fade + jnp.sum(e1, axis=0, keepdims=True))
            fade = fade * inv
            p2 = e_ref[u, :rows] * fade
            p1 = e1 * inv
            p0 = e_ref[u, rows:] * fade
            p_ref[u, :rows] = p2
            p_ref[u, rows:WINDOW_SIZE] = p1
            p_ref[u, WINDOW_SIZE:] = p0
            low_ref[u] = p0.astype(BF16)
            g1v_ref[:, columns(u)] = dot(p1.astype(BF16), go_ref[u], 1, 0).astype(BF16)
            g2v_ref[:, columns(u)] = dot(p2.astype(BF16), go_ref[u], 1, 0).astype(BF16)


def score_kernel(p_ref, low_ref, v0_ref, v1_ref, v2_ref, go_ref, got_ref, dp_ref, qh_ref, qn_ref, kn2_ref, kn1_ref, kn0_ref,
                 kg_ref, g1k_ref, g2k_ref, ds_ref, dqn_ref, gains_ref):
    rows = v0_ref.shape[0]
    q_part = jnp.zeros((1, HEAD_SIZE), F32)
    k_part = jnp.zeros((1, HEAD_SIZE), F32)
    ready = {}
    for turn in range(KEY_VALUE_HEADS + 2):
        u = turn
        if u < KEY_VALUE_HEADS:
            v = jnp.concatenate([v2_ref[:, columns(u)], v1_ref[:, columns(u)]], axis=0)
            p, p0 = p_ref[u, :WINDOW_SIZE], p_ref[u, WINDOW_SIZE:]
            attended = dot(v, p.astype(BF16), 0, 0) + dot(v0_ref[:, columns(u)], low_ref[u], 0, 0)
            attended = attended.astype(BF16).astype(F32)
            delta = jnp.sum(got_ref[u].astype(F32) * attended, axis=0, keepdims=True)
            ds = (p * (dot(v, go_ref[u], 1, 1) - delta)).astype(BF16)
            ds0 = (p0 * (dp_ref[u] - delta)).astype(BF16)
            ds_ref[u] = ds0
            ready[u] = (ds, ds0)
        u = turn - 2
        if u >= 0:
            ds, ds0 = ready.pop(u)
            qn = qn_ref[u]
            g = (dot(ds, qn, 1, 0) * score_scale).astype(BF16)
            g2k_ref[:, columns(u)] = g[:rows]
            g1k_ref[:, columns(u)] = g[rows:]
            kn = jnp.concatenate([ref[:, columns(u)] for ref in (kn2_ref, kn1_ref, kn0_ref)], axis=0)
            dqn = jnp.transpose(dot(kn, jnp.concatenate([ds, ds0], axis=0), 0, 0)) * score_scale
            dqn_ref[u] = dqn
            q_part = q_part + jnp.sum(dqn * qh_ref[u], axis=0, keepdims=True)
            k_part = k_part + jnp.sum(dqn * qn.astype(F32), axis=0, keepdims=True)
    parts = jnp.concatenate([q_part, k_part / kg_ref[...]], axis=0)
    gains_ref[...] = jnp.broadcast_to(parts[None], gains_ref.shape)


def rest_kernel(q_ref, go_ref, low_ref, ds_ref, dqn_ref, qg_ref, a_ref, b_ref,
                dq_ref, dk_ref, dv_ref):
    rows = a_ref.shape[0]
    for u in range(KEY_VALUE_HEADS):
        own = dot(low_ref[u], stacked(go_ref, u), 1, 0)
        total = own + a_ref[:, columns(u)].astype(F32) + b_ref[:, columns(u)].astype(F32)
        dv_ref[:, columns(u)] = total.astype(BF16)
        q = stacked(q_ref, u).astype(F32)
        q_inv = inverse_rms(q)
        q_hat = q * q_inv
        dk_ref[:, columns(u)] = dot(ds_ref[u], (q_hat * qg_ref[...]).astype(BF16), 1, 0) * score_scale
        t = dqn_ref[u] * qg_ref[...]
        dq = (q_inv * (t - q_hat * jnp.mean(t * q_hat, axis=-1, keepdims=True))).astype(BF16)
        for i in range(GROUP):
            dq_ref[:, columns(u * GROUP + i)] = dq[i * rows:(i + 1) * rows]


def turn_kernel(odd_ref, own_ref, got_ref, out_ref):
    out_ref[...] = jnp.where(odd_ref[0] == 1, got_ref[...], own_ref[...])


def join_kernel(odd_ref, own_ref, got_ref, out_ref):
    keep = (odd_ref[0] == 1).astype(F32)
    out_ref[...] = (own_ref[...].astype(F32) + got_ref[...].astype(F32) * keep).astype(BF16)


def total_kernel(k_ref, parts_ref, q_out_ref, k_out_ref, kh_ref, ki_ref):
    total = jnp.sum(parts_ref[...], axis=0)
    q_out_ref[...] = total[0:1]
    k_out_ref[...] = total[1:2]
    for u in range(KEY_VALUE_HEADS):
        k = k_ref[:, columns(u)].astype(F32)
        k_inv = inverse_rms(k)
        kh_ref[:, columns(u)] = k * k_inv
        ki_ref[:, columns(u)] = jnp.broadcast_to(k_inv, k.shape)


def key_kernel(odd_ref, kh_ref, ki_ref, dk_ref, a_ref, b_ref, kg_ref, out_ref):
    keep = (odd_ref[0] == 0).astype(F32)
    for u in range(KEY_VALUE_HEADS):
        total = dk_ref[:, columns(u)] + a_ref[:, columns(u)].astype(F32) * keep + b_ref[:, columns(u)].astype(F32)
        k_hat = kh_ref[:, columns(u)]
        t = total * kg_ref[...]
        dk = ki_ref[:, columns(u)] * (t - k_hat * jnp.mean(t * k_hat, axis=-1, keepdims=True))
        out_ref[:, columns(u)] = dk.astype(BF16)


def call(kernel, outs, args, scalars=()):
    vmem = pl.BlockSpec(memory_space=pltpu.VMEM)
    return pl.pallas_call(
        kernel,
        in_specs=[pl.BlockSpec(memory_space=pltpu.SMEM)] * len(scalars) + [vmem] * len(args),
        out_specs=[vmem] * len(outs),
        out_shape=outs,
        compiler_params=pltpu.CompilerParams(vmem_limit_bytes=VMEM_LIMIT),
    )(*scalars, *args)


def near(*arrays):
    return tuple(pltpu.with_memory_space_constraint(array, pltpu.VMEM) for array in arrays)


def far(*arrays):
    return tuple(pltpu.with_memory_space_constraint(array, pltpu.HBM) for array in arrays)


def per_device(queries, keys, values, grad_out, query_gain, key_gain, doc_lengths):
    rows = queries.shape[1]
    count = lax.axis_size("ctx")
    assert rows * 2 == WINDOW_SIZE and count % 2 == 0
    here = lax.axis_index("ctx")
    odd = lax.rem(here, 2)
    first = (here * rows).astype(jnp.int32)
    q, k, v, go = queries[0], keys[0], values[0], grad_out[0]
    q_gain, k_gain = query_gain[None], key_gain[None]

    ahead = [(i, (i + 2) % count) for i in range(count)]
    behind = [(i, (i - 2) % count) for i in range(count)]
    follow = [(i, (i + 1) % count) for i in range(count)]
    lead = [(i, (i - 1) % count) for i in range(count)]
    swap = [(i, i ^ 1) for i in range(count)]

    pair, keys, heads = GROUP * rows, WINDOW_SIZE + rows, KEY_VALUE_HEADS
    flat = (rows, heads * HEAD_SIZE)
    devices = count * lax.axis_size("dp")
    parity = odd.astype(jnp.int32)[None]

    held, away = pltpu.VMEM, jax.ShapeDtypeStruct
    k2 = lax.ppermute(k, "ctx", ahead)
    q_hat, qn, kn0, s0, dp0, go2, go_t, v0, bias, k0, qg, kg = call(
        prepare_kernel,
        [
            held((heads, pair, HEAD_SIZE), F32),
            held((heads, pair, HEAD_SIZE), BF16), held(flat, BF16),
            held((heads, rows, pair), F32), held((heads, rows, pair), F32),
            held((heads, pair, HEAD_SIZE), BF16), held((heads, HEAD_SIZE, pair), BF16),
            held(flat, BF16), held((WINDOW_SIZE, rows), F32), held(flat, BF16),
            held((1, HEAD_SIZE), F32), held((1, HEAD_SIZE), F32),
        ],
        far(q, k, v, go, q_gain, k_gain), (first[None],) + far(doc_lengths),
    )
    turned = call(turn_kernel, [held(flat, BF16)], near(k0, k2), (parity,))[0]
    k1 = lax.ppermute(turned, "ctx", swap)
    v2 = lax.ppermute(v, "ctx", ahead)
    v1 = lax.ppermute(v, "ctx", follow[:-1])

    kn2, e, top, norm = call(
        early_kernel,
        [
            held(flat, BF16), held((heads, WINDOW_SIZE, pair), F32),
            held((heads, 1, pair), F32), held((heads, 1, pair), F32),
        ],
        near(qn, s0, bias, k2, kg),
    )
    kn1, p, p_low, g1v, g2v = call(
        weigh_kernel,
        [
            held(flat, BF16), held((heads, keys, pair), F32), held((heads, rows, pair), BF16),
            held(flat, BF16), held(flat, BF16),
        ],
        near(qn, e, top, norm, bias, k1, go2, kg),
    )
    av = lax.ppermute(g1v, "ctx", lead[1:])
    bv = lax.ppermute(g2v, "ctx", behind)

    g1k, g2k, ds0, dqn, gains = call(
        score_kernel,
        [
            held(flat, BF16), held(flat, BF16), held((heads, rows, pair), BF16),
            held((heads, pair, HEAD_SIZE), F32), held((devices, 2, HEAD_SIZE), F32),
        ],
        near(p, p_low, v0, v1, v2, go2, go_t, dp0, q_hat, qn, kn2, kn1, kn0, kg),
    )
    ak = lax.ppermute(g1k, "ctx", swap)
    joined = call(join_kernel, [held(flat, BF16)], near(g2k, ak), (parity,))[0]
    bk = lax.ppermute(joined, "ctx", behind)
    spread = lax.all_to_all(gains, ("ctx", "dp"), 0, 0)
    line = away((1, HEAD_SIZE), F32)
    q_total, k_total, k_hat, k_inv = call(
        total_kernel, [line, line, held(flat, F32), held(flat, F32)], far(k) + near(spread)
    )

    dq, dk_own, dv = call(
        rest_kernel, [away(q.shape, BF16), held(flat, F32), away(flat, BF16)],
        far(q, go) + near(p_low, ds0, dqn, qg) + far(av, bv),
    )
    dk = call(
        key_kernel, [away(flat, BF16)],
        near(k_hat, k_inv, dk_own, ak, bk, kg), (parity,),
    )[0]
    return (dq[None], dk[None], dv[None], q_total[0], k_total[0])


def solution(mesh):
    in_specs = (
        P("dp", "ctx", None),
        P("dp", "ctx", None),
        P("dp", "ctx", None),
        P("dp", "ctx", None),
        P(),
        P(),
        P("dp", None),
    )
    out_specs = (P("dp", "ctx", None), P("dp", "ctx", None), P("dp", "ctx", None), P(), P())
    return jax.shard_map(
        per_device, mesh=mesh, in_specs=in_specs, out_specs=out_specs, check_vma=False
    )
```
